512 devices in a mesh: grp: 2 (over core), gx: 16 (over x_hi, y), gy: 16 (over x_lo, z).
Axes of the slice: x: 4 (x_hi: 2, x_lo: 2; x = x_hi * 2 + x_lo), y: 8, z: 8, core: 2. Of those that a mesh axis runs over, the one named last changes fastest.
Arguments:
- state_now: float32 [2, 128, 256, 256], P('grp', 'gx', 'gy'), may hold values from -6 to 6
- state_later: float32 [2, 128, 256, 256], P('grp', 'gx', 'gy'), may hold values from -6 to 6
- courant: float32 [128, 256, 256], P('gx', 'gy'), may hold values from 0.04 to 0.18
- strips: float32 [8, 128, 2048], P(None, 'gx', 'gy'), may hold values from -6 to 6
- traces: float32 [8, 16, 16, 128], P(None, 'gx', 'gy'), may hold values from -60 to 60
- receiver_cells: int32 [16, 16, 128], P('gx', 'gy'), may hold values from 0 to 32767
- source_point: int32 [3], replicated, may hold values from 0 to 127
- wavelet: float32 [8], replicated, may hold values from -100 to 100
Outputs:
- image_sum: float32 [128, 256, 256], P('gx', 'gy', 'grp')
- wave_now: float32 [2, 128, 256, 256], P('grp', 'gx', 'gy')
- wave_later: float32 [2, 128, 256, 256], P('grp', 'gx', 'gy')
The draws below stay inside these ranges and needn't reach their ends.
Inputs may be any that keep to these rules, and one draw needn't show every extreme that they name: `receiver_cells`: index of the cell in its block, depth fastest, then crossline, then inline; several receivers may share a cell.
All inputs are finite; a program needn't handle non-finite values.
Results may differ from the reference program's by a relative error of at most 0.00002.
Values sent between devices are 32-bit elements; how exact they have to be, the bound alone decides.
A program may use at most 64 MiB of HBM per device.

```python
import math
import jax
import jax.numpy as jnp

CX = 8
CY = 16
CZ = 256
RPD = 128
STEPS = 8
GROUPS = 2
TILES_X = 16
TILES_Y = 16
NX = 128
NY = 256
NZ = 256
N_GX = 16
N_GY = 16


def plant(drawn, own_key, least, high):
    longest = drawn.shape.index(max(drawn.shape))
    spots = []
    for shift in (0, 1):
        where = [jax.random.randint(jax.random.fold_in(own_key, axis), (), 0, length) for axis, length in enumerate(drawn.shape)]
        where[longest] = (where[longest] + shift) % drawn.shape[longest]
        spots.append(tuple(where))
    return drawn.at[spots[0]].set(least).at[spots[1]].set(high)


def block_levels(own_key, extent, split, smallest, top_value):
    def one(axis_at, blocks):
        heights = jax.random.uniform(jax.random.fold_in(jax.random.fold_in(own_key, 6), axis_at), (blocks,), jnp.float32, smallest / len(split), top_value / len(split))
        return jnp.repeat(jnp.exp(heights), extent[axis_at] // blocks).reshape((-1,) + (1,) * (len(extent) - axis_at - 1))

    gain = one(*split[0])
    for cut in split[1:]:
        gain = gain * one(*cut)
    return gain


def gaussian(stream_key, shape, deviation, reach, cuts=(), kind=jnp.bfloat16):
    array = jax.random.normal(stream_key, shape, jnp.float32) * deviation
    if len(cuts) > 0:
        array = block_levels(stream_key, shape, cuts, -0.22, 0.18) * array
    return jnp.clip(array, min=-reach, max=reach).astype(kind)


def setup_inputs(seed: int = 0) -> dict:
    streams_of = jax.random.split(jax.random.key(seed), 9)
    state_now = gaussian(streams_of[0], (GROUPS, NX, NY, NZ), 1.0, 6.0, ((0, 2), (1, 16), (2, 16)), jnp.float32)
    state_later = gaussian(streams_of[1], (GROUPS, NX, NY, NZ), 1.0, 6.0, ((0, 2), (1, 16), (2, 16)), jnp.float32)
    courant = jnp.clip(jnp.exp(math.log(0.18) - 1.50407746 * jax.random.uniform(streams_of[2], (NX, NY, NZ), jnp.float32) ** block_levels(streams_of[2], (NX, NY, NZ), ((0, 16), (1, 16)), -0.2, 0.2)), 0.04, 0.18)
    strips = gaussian(streams_of[3], (STEPS, NX, NY * 8), 1.0, 6.0, ((1, 16), (2, 16)), jnp.float32)
    traces = gaussian(streams_of[4], (STEPS, TILES_X, TILES_Y, RPD), 10.0, 60.0, ((1, 16), (2, 16)), jnp.float32)
    receiver_cells = plant(jax.random.randint(streams_of[5], (TILES_X, TILES_Y, RPD), 0, CX * CY * CZ), jax.random.fold_in(streams_of[5], 1), 0, (CX * CY * CZ) - 1).astype(jnp.int32)
    source_point = jax.random.randint(streams_of[6], (3,), 0, min(NX, min(NY, NZ))).astype(jnp.int32)
    wavelet = gaussian(streams_of[7], (STEPS,), 20.0, 100.0, (), jnp.float32)
    return dict(state_now=state_now, state_later=state_later, courant=courant, strips=strips, traces=traces, receiver_cells=receiver_cells, source_point=source_point, wavelet=wavelet)


STENCIL = (-205.0 / 72.0, 8.0 / 5.0, -1.0 / 5.0, 8.0 / 315.0, -1.0 / 560.0)


def laplacian(padded):
    span_x = padded.shape[-3] - 8
    span_y = padded.shape[-2] - 8
    span_z = padded.shape[-1] - 8

    def window(offset_x, offset_y, offset_z):
        return padded[..., 4 + offset_x:4 + offset_x + span_x, 4 + offset_y:4 + offset_y + span_y, 4 + offset_z:4 + offset_z + span_z]

    accumulated = (3.0 * STENCIL[0]) * window(0, 0, 0)
    for radius in range(1, 5):
        beside_all = window(radius, 0, 0) + window(-radius, 0, 0) + window(0, radius, 0) + window(0, -radius, 0) + window(0, 0, radius) + window(0, 0, -radius)
        accumulated = accumulated + STENCIL[radius] * beside_all
    return accumulated


def reference(state_now, state_later, courant, strips, traces, receiver_cells, source_point, wavelet):
    current = state_now
    future = state_later
    depth_idx = jnp.arange(NZ, dtype=jnp.int32)
    strip_layer = ((depth_idx < 4) | (depth_idx >= NZ - 4))[None, None, :]
    tile_x = jnp.arange(N_GX, dtype=jnp.int32)[:, None, None]
    tile_y = jnp.arange(N_GY, dtype=jnp.int32)[None, :, None]
    local_x = receiver_cells // (CY * CZ)
    local_y = (receiver_cells // CZ) % CY
    local_z = receiver_cells % CZ
    flat_cells = (((tile_x * CX + local_x) * NY + tile_y * CY + local_y) * NZ + local_z).reshape(-1).astype(jnp.int32)
    courant_flat = courant.reshape(-1)
    receiver_coef = courant_flat[flat_cells]
    source_flat = ((source_point[0] * NY + source_point[1]) * NZ + source_point[2]).astype(jnp.int32)
    source_coef = courant_flat[source_flat]
    strip_cells = strips.reshape(STEPS, NX, NY, 8)
    filler = jnp.zeros((NX, NY, NZ - 8), jnp.float32)
    image_sum = jnp.zeros((NX, NY, NZ), jnp.float32)
    for moment in range(STEPS):
        padded = jnp.pad(current, ((0, 0), (4, 4), (4, 4), (4, 4)))
        computed = 2.0 * current - future + courant[None] * laplacian(padded)
        receiver_add = jnp.zeros((NX * NY * NZ,), jnp.float32).at[flat_cells].add(receiver_coef * traces[moment].reshape(-1)).reshape(NX, NY, NZ)
        source_add = jnp.zeros((NX * NY * NZ,), jnp.float32).at[source_flat].add(-source_coef * wavelet[moment]).reshape(NX, NY, NZ)
        strip_dense = jnp.concatenate([strip_cells[moment][..., :4], filler, strip_cells[moment][..., 4:]], axis=-1)
        source_new = jnp.where(strip_layer, strip_dense, computed[0] + source_add)
        receiver_new = computed[1] + receiver_add
        newest = jnp.stack([source_new, receiver_new])
        future = current
        current = newest
        if (moment + 1) % 4 == 0:
            image_sum = image_sum + newest[0] * newest[1]
    return image_sum, current, future
```

```python
import jax
import jax.numpy as jnp
from jax import lax
from jax.experimental import pallas as pl
from jax.experimental.pallas import tpu as pltpu
from jax.sharding import PartitionSpec as P

STEPS = 8
STENCIL = (-205.0 / 72.0, 8.0 / 5.0, -1.0 / 5.0, 8.0 / 315.0, -1.0 / 560.0)
MESH = pl.DeviceIdType.MESH
F32 = jnp.float32
BF16 = jnp.bfloat16


def split3(value):
    high = value.astype(BF16).astype(F32)
    rest = value - high
    middle = rest.astype(BF16).astype(F32)
    return high, middle, rest - middle


def shifted_sum(lower, upper, k, lane):
    lower_up, upper_up = pltpu.roll(lower, k, 1), pltpu.roll(upper, k, 1)
    lower_down, upper_down = pltpu.roll(lower, 128 - k, 1), pltpu.roll(upper, 128 - k, 1)
    zero = jnp.zeros_like(lower)
    first, last = lane >= k, lane < 128 - k
    return (
        jnp.where(first, lower_up, zero) + jnp.where(last, lower_down, upper_down),
        jnp.where(first, upper_up, lower_up) + jnp.where(last, upper_down, zero),
    )


def kernel(
    now, later, courant, strips, traces, cells, source, wavelet,
    image_out, now_out, later_out,
    u, xr, yr, ys, yl, yh, c, t, acc_inj, dense, image_in, image, strip_v, trace_v, cell_v,
    load_sem, xs_sem, xr_sem, ysend_sem, yr_sem, im_send, im_recv, out_sem,
):
    a0, a1, a2, a3, a4 = STENCIL
    weights = (a1, a2, a3, a4)
    group = lax.axis_index("grp")
    at_x = lax.axis_index("gx")
    at_y = lax.axis_index("gy")
    size_x = lax.axis_size("gx")
    size_y = lax.axis_size("gy")
    source_side = group == 0
    has_x = (at_x > 0, at_x < size_x - 1)
    has_y = (at_y > 0, at_y < size_y - 1)
    to_x = ({"gx": at_x - 1}, {"gx": at_x + 1})
    to_y = ({"gy": at_y - 1}, {"gy": at_y + 1})
    partner = {"grp": 1 - group}

    loads = []
    for h in range(2):
        zs = pl.ds(128 * h, 128)
        loads.append(pltpu.make_async_copy(now.at[0, :, :, zs], u.at[0, h, :, pl.ds(8, 16)], load_sem.at[h]))
        loads.append(pltpu.make_async_copy(later.at[0, :, :, zs], u.at[1, h, :, pl.ds(8, 16)], load_sem.at[2 + h]))
        loads.append(pltpu.make_async_copy(courant.at[:, :, zs], c.at[h], load_sem.at[4 + h]))
    loads.append(pltpu.make_async_copy(strips, strip_v, load_sem.at[6]))
    loads.append(pltpu.make_async_copy(traces, trace_v, load_sem.at[7]))
    loads.append(pltpu.make_async_copy(cells, cell_v, load_sem.at[8]))
    for copy in loads:
        copy.start()

    zero8 = jnp.zeros((2, 2, 8, 8, 128), F32)
    u[:, :, :, 0:8] = zero8
    u[:, :, :, 24:32] = zero8
    xr[...] = jnp.zeros_like(xr)
    yr[...] = jnp.zeros_like(yr)
    yl[...] = jnp.zeros_like(yl)
    yh[...] = jnp.zeros_like(yh)

    barrier = pltpu.get_barrier_semaphore()
    count = jnp.int32(1)
    pl.semaphore_signal(barrier, inc=1, device_id=partner, device_id_type=MESH)
    for d in range(2):
        count = count + has_x[d].astype(jnp.int32) + has_y[d].astype(jnp.int32)

        @pl.when(has_x[d])
        def _():
            pl.semaphore_signal(barrier, inc=1, device_id=to_x[d], device_id_type=MESH)

        @pl.when(has_y[d])
        def _():
            pl.semaphore_signal(barrier, inc=1, device_id=to_y[d], device_id_type=MESH)

    pl.semaphore_wait(barrier, count)

    def x_copy(par, d):
        return pltpu.make_async_remote_copy(
            src_ref=u.at[par, :, pl.ds(4 * d, 4), pl.ds(8, 16)],
            dst_ref=xr.at[par, 1 - d],
            send_sem=xs_sem.at[par, d],
            recv_sem=xr_sem.at[par, 1 - d],
            device_id=to_x[d],
            device_id_type=MESH,
        )

    def y_copy(par, d):
        return pltpu.make_async_remote_copy(
            src_ref=ys.at[par, d],
            dst_ref=yr.at[par, 1 - d],
            send_sem=ysend_sem.at[par, d],
            recv_sem=yr_sem.at[par, 1 - d],
            device_id=to_y[d],
            device_id_type=MESH,
        )

    def image_copy(slot):
        par = 0
        return pltpu.make_async_remote_copy(
            src_ref=u.at[par, 1 - group, :, pl.ds(8, 16)],
            dst_ref=image_in.at[slot],
            send_sem=im_send.at[slot],
            recv_sem=im_recv.at[slot],
            device_id=partner,
            device_id_type=MESH,
        )

    for copy in loads[:2] + loads[3:5]:
        pass
    loads[0].wait()
    loads[3].wait()
    for d in range(2):

        @pl.when(has_x[d])
        def _():
            x_copy(0, d).start()

    for d in range(2):
        ys[0, d] = u[0, :, :, 8 + 12 * d : 12 + 12 * d]

        @pl.when(has_y[d])
        def _():
            y_copy(0, d).start()

    for i in (1, 2, 4, 5, 6, 7, 8):
        loads[i].wait()

    lane = lax.broadcasted_iota(jnp.int32, (16, 128), 1)
    lane1 = lax.broadcasted_iota(jnp.int32, (1, 128), 1)
    source_x = source[0] - at_x * 8
    source_y = source[1] - at_y * 16
    inside = (source_x >= 0) & (source_x < 8) & (source_y >= 0) & (source_y < 16)
    source_flat = jnp.where(inside, (source_x * 16 + source_y) * 256 + source[2], -1)
    where_to = jnp.where(source_side, jnp.where(lane1 == 0, source_flat, -1), cell_v[0])
    row_of = jnp.where(where_to < 0, -1, ((where_to >> 7) & 1) * 128 + (where_to >> 8))
    column_of = where_to & 127
    column_hot = jnp.where(
        lax.broadcasted_iota(jnp.int32, (128, 128), 0) == column_of, 1.0, 0.0
    ).astype(BF16)
    row_hot = lax.broadcasted_iota(jnp.int32, (256, 128), 0) == row_of
    from_entry = lax.broadcasted_iota(jnp.int32, (128, 256), 0)
    to_depth = lax.broadcasted_iota(jnp.int32, (128, 256), 1)
    layer = from_entry & 7
    depth_of = jnp.where(layer < 4, layer, 248 + layer)
    spread = jnp.where(to_depth == depth_of, 1.0, 0.0).astype(BF16)
    own_row = (
        lax.broadcasted_iota(jnp.int32, (8, 16, 128), 2) >> 3
        == lax.broadcasted_iota(jnp.int32, (8, 16, 128), 1)
    )
    overwrite = (
        jnp.logical_and(lane < 4, source_side),
        jnp.logical_and(lane >= 124, source_side),
    )

    def prepare(par, k):
        sample = jnp.where(
            source_side, jnp.where(lane1 == 0, -wavelet[k], 0.0), trace_v[k, 0]
        )
        inject = jnp.zeros((256, 128), F32)
        for part in split3(sample):
            left = jnp.where(row_hot, part, 0.0).astype(BF16)
            inject = inject + lax.dot_general(
                left, column_hot, (((1,), (1,)), ((), ())), preferred_element_type=F32
            )
        acc_inj[...] = inject.reshape(2, 8, 16, 128)
        strip = jnp.zeros((128, 256), F32)
        for part in split3(strip_v[k]):
            left = jnp.where(own_row, part[:, None, :], 0.0).reshape(128, 128).astype(BF16)
            strip = strip + jnp.dot(left, spread, preferred_element_type=F32)
        for h in range(2):
            dense[h] = strip[:, 128 * h : 128 * h + 128].reshape(8, 16, 128)

        for x in range(8):
            for h in range(2):
                own = u[par, h, x, 8:24]
                total = acc_inj[h, x] + (3.0 * a0) * own
                for k_ in range(1, 5):
                    near = u[par, h, x, 8 - k_ : 24 - k_] + u[par, h, x, 8 + k_ : 24 + k_]
                    if x - k_ >= 0:
                        near = near + u[par, h, x - k_, 8:24]
                    if x + k_ < 8:
                        near = near + u[par, h, x + k_, 8:24]
                    total = total + weights[k_ - 1] * near
                acc_inj[h, x] = total
            lower, upper = u[par, 0, x, 8:24], u[par, 1, x, 8:24]
            sums = [acc_inj[0, x], acc_inj[1, x]]
            for k_ in range(1, 5):
                both = shifted_sum(lower, upper, k_, lane)
                for h in range(2):
                    sums[h] = sums[h] + weights[k_ - 1] * both[h]
            for h in range(2):
                value = 2.0 * (lower, upper)[h] - u[1 - par, h, x, 8:24] + c[h, x] * sums[h]
                t[h, x] = jnp.where(overwrite[h], dense[h, x], value)

    for x in range(8):
        for h in range(2):
            pass

    def y_halo(par, x, h):
        low = jnp.zeros((8, 128), F32)
        high = jnp.zeros((8, 128), F32)
        for m in range(4):
            low = low + weights[3 - m] * yl[h, x, m : m + 8]
            high = high + weights[3 - m] * yh[h, x, 4 - m : 12 - m]
        return low, high

    def finish(par, k, more):
        for d in range(2):

            @pl.when(has_y[d])
            def _():
                y_copy(par, 1 - d).wait_recv()

        for x in range(8):
            yl[:, x, 0:4] = yr[par, 0, :, x]
            yh[:, x, 8:12] = yr[par, 1, :, x]

        new = 1 - par
        for d in range(2):

            @pl.when(has_x[d])
            def _():
                x_copy(par, 1 - d).wait_recv()

            for x in range(4 * d, 4 * d + 4):
                for h in range(2):
                    extra = None
                    for j in range(4):
                        distance = x + 4 - j if d == 0 else 8 + j - x
                        if distance <= 4:
                            term = weights[distance - 1] * xr[par, d, h, j]
                            extra = term if extra is None else extra + term
                    low, high = y_halo(par, x, h)
                    cx = jnp.where(overwrite[h], 0.0, c[h, x])
                    first = t[h, x, 0:8] + cx[0:8] * (extra[0:8] + low)
                    second = t[h, x, 8:16] + cx[8:16] * (extra[8:16] + high)
                    u[new, h, x, 8:16] = first
                    u[new, h, x, 16:24] = second
                    ys[new, 0, h, x] = first[0:4]
                    ys[new, 1, h, x] = second[4:8]

            @pl.when(jnp.logical_and(more, has_x[d]))
            def _():
                x_copy(new, d).start()

        for d in range(2):

            @pl.when(jnp.logical_and(more, has_y[d]))
            def _():
                y_copy(new, d).start()

    def sent(par):
        for d in range(2):

            @pl.when(has_x[d])
            def _():
                x_copy(par, d).wait_send()

            @pl.when(has_y[d])
            def _():
                y_copy(par, d).wait_send()

    def four(half, carry):
        for s in range(4):
            k = 4 * half + s
            par = s % 2
            if s == 0:

                @pl.when(half == 1)
                def _():
                    image_copy(0).wait()
                    image[...] = u[0, group, :, 8:24] * image_in[0]

            prepare(par, k)
            if s == 0:

                @pl.when(half == 1)
                def _():
                    sent(1)

            else:
                sent(1 - par)
            finish(par, k, True if s < 3 else half == 0)
            if s == 3:

                @pl.when(half == 0)
                def _():
                    image_copy(0).start()

                @pl.when(half == 1)
                def _():
                    image_copy(1).start()

        return carry

    lax.fori_loop(0, 2, four, 0)
    outs = []
    for h in range(2):
        zs = pl.ds(128 * h, 128)
        outs.append(pltpu.make_async_copy(u.at[1, h, :, pl.ds(8, 16)], later_out.at[0, :, :, zs], out_sem.at[h]))
        outs.append(pltpu.make_async_copy(u.at[0, h, :, pl.ds(8, 16)], now_out.at[0, :, :, zs], out_sem.at[2 + h]))
    for copy in outs:
        copy.start()
    sent(1)
    image_copy(1).wait()
    image[...] = image[...] + u[0, group, :, 8:24] * image_in[1]
    last = pltpu.make_async_copy(image, image_out, out_sem.at[4])
    last.start()
    for copy in outs:
        copy.wait()
    last.wait()


def local(state_now, state_later, courant, strips, traces, receiver_cells, source_point, wavelet):
    any_space = pl.BlockSpec(memory_space=pl.ANY)
    smem = pl.BlockSpec(memory_space=pltpu.SMEM)
    dma = pltpu.SemaphoreType.DMA
    return pl.pallas_call(
        kernel,
        out_shape=(
            jax.ShapeDtypeStruct((8, 16, 128), F32),
            jax.ShapeDtypeStruct((1, 8, 16, 256), F32),
            jax.ShapeDtypeStruct((1, 8, 16, 256), F32),
        ),
        in_specs=[any_space] * 6 + [smem] * 2,
        out_specs=(any_space,) * 3,
        scratch_shapes=[
            pltpu.VMEM((2, 2, 8, 32, 128), F32),
            pltpu.VMEM((2, 2, 2, 4, 16, 128), F32),
            pltpu.VMEM((2, 2, 2, 8, 4, 128), F32),
            pltpu.VMEM((2, 2, 2, 8, 4, 128), F32),
            pltpu.VMEM((2, 8, 16, 128), F32),
            pltpu.VMEM((2, 8, 16, 128), F32),
            pltpu.VMEM((2, 8, 16, 128), F32),
            pltpu.VMEM((2, 8, 16, 128), F32),
            pltpu.VMEM((2, 8, 16, 128), F32),
            pltpu.VMEM((2, 8, 16, 128), F32),
            pltpu.VMEM((2, 8, 16, 128), F32),
            pltpu.VMEM((8, 16, 128), F32),
            pltpu.VMEM((8, 8, 128), F32),
            pltpu.VMEM((8, 1, 1, 128), F32),
            pltpu.VMEM((1, 1, 128), jnp.int32),
            dma((9,)),
            dma((2, 2)),
            dma((2, 2)),
            dma((2, 2)),
            dma((2, 2)),
            dma((2,)),
            dma((2,)),
            dma((5,)),
        ],
        compiler_params=pltpu.CompilerParams(collective_id=0, has_side_effects=True),
    )(state_now, state_later, courant, strips, traces, receiver_cells, source_point, wavelet)


def solution(mesh):
    in_specs = (
        P("grp", "gx", "gy", None),
        P("grp", "gx", "gy", None),
        P("gx", "gy", None),
        P(None, "gx", "gy"),
        P(None, "gx", "gy", None),
        P("gx", "gy", None),
        P(),
        P(),
    )
    out_specs = (P("gx", "gy", "grp"), P("grp", "gx", "gy", None), P("grp", "gx", "gy", None))
    return jax.shard_map(local, mesh=mesh, in_specs=in_specs, out_specs=out_specs, check_vma=False)
```

```python
import jax
import jax.numpy as jnp
from jax import lax
from jax.experimental import pallas as pl
from jax.experimental.pallas import tpu as pltpu
from jax.sharding import PartitionSpec as P

STENCIL = (-205.0 / 72.0, 8.0 / 5.0, -1.0 / 5.0, 8.0 / 315.0, -1.0 / 560.0)
W = (None,) + STENCIL[1:]
MESH = pl.DeviceIdType.MESH
F32 = jnp.float32
BF16 = jnp.bfloat16


def split3(value):
    high = value.astype(BF16).astype(F32)
    rest = value - high
    middle = rest.astype(BF16).astype(F32)
    return high, middle, rest - middle


def shifted_sum(lower, upper, k, lane):
    lower_up, upper_up = pltpu.roll(lower, k, 1), pltpu.roll(upper, k, 1)
    lower_down, upper_down = pltpu.roll(lower, 128 - k, 1), pltpu.roll(upper, 128 - k, 1)
    zero = jnp.zeros_like(lower)
    first, last = lane >= k, lane < 128 - k
    return (
        jnp.where(first, lower_up, zero) + jnp.where(last, lower_down, upper_down),
        jnp.where(first, upper_up, lower_up) + jnp.where(last, upper_down, zero),
    )


def add(total, term):
    return term if total is None else total + term


def kernel(
    now, later, courant, strips, traces, cells, source_in, wavelet_in,
    image_out, now_out, later_out,
    u, t, c, cm, xr, xtr, yr, ytr, cr, xc, yc, xcm, ycm, ys, yts, ycs,
    yl, yh, cl, ch, hx, hy, inj, dense, image_in, image,
    strip_v, trace_v, cell_v, source, wavelet,
    load_sem, xs_sem, xts_sem, ys_sem, yts_sem, cs_sem, xcs_sem, ycs_sem,
    xr_sem, xtr_sem, yr_sem, ytr_sem, cr_sem, xcr_sem, ycr_sem, im_send, im_recv,
):
    group = lax.axis_index("grp")
    at_x = lax.axis_index("gx")
    at_y = lax.axis_index("gy")
    size_x = lax.axis_size("gx")
    size_y = lax.axis_size("gy")
    source_side = group == 0
    has_x = (at_x > 0, at_x < size_x - 1)
    has_y = (at_y > 0, at_y < size_y - 1)
    x_of = (at_x - 1, at_x + 1)
    y_of = (at_y - 1, at_y + 1)
    partner = {"grp": 1 - group}
    corners = [(i, j) for i in range(2) for j in range(2)]
    has_c = {(i, j): jnp.logical_and(has_x[i], has_y[j]) for i, j in corners}

    barrier = pltpu.get_barrier_semaphore()
    count = jnp.int32(1)
    others = [(has_x[d], {"gx": x_of[d]}) for d in range(2)]
    others += [(has_y[d], {"gy": y_of[d]}) for d in range(2)]
    others += [(has_c[i, j], {"gx": x_of[i], "gy": y_of[j]}) for i, j in corners]
    pl.semaphore_signal(barrier, inc=1, device_id=partner, device_id_type=MESH)
    for there, device in others:
        count = count + there.astype(jnp.int32)

        @pl.when(there)
        def _():
            pl.semaphore_signal(barrier, inc=1, device_id=device, device_id_type=MESH)

    loads = []
    for h in range(2):
        zs = pl.ds(128 * h, 128)
        loads.append((now.at[0, :, :, zs], u.at[0, h, :, pl.ds(8, 16)]))
        loads.append((later.at[0, :, :, zs], u.at[1, h, :, pl.ds(8, 16)]))
        loads.append((courant.at[:, :, zs], c.at[h]))
    loads += [(cells, cell_v), (traces, trace_v), (strips, strip_v)]
    loads += [(source_in, source), (wavelet_in, wavelet)]
    loads = [pltpu.make_async_copy(a, b, load_sem.at[i]) for i, (a, b) in enumerate(loads)]
    for copy in loads:
        copy.start()

    for slot in range(2):
        u[slot, :, :, 0:8] = jnp.zeros((2, 8, 8, 128), F32)
        u[slot, :, :, 24:32] = jnp.zeros((2, 8, 8, 128), F32)
    for ref in (yl, yh, cl, ch):
        ref[...] = jnp.zeros_like(ref)
    for d in range(2):

        @pl.when(jnp.logical_not(has_x[d]))
        def _():
            xc[d] = jnp.zeros_like(xc[d])
            for par in range(2):
                xr[par, d] = jnp.zeros_like(xr[par, d])
                xtr[par, d] = jnp.zeros_like(xtr[par, d])

        @pl.when(jnp.logical_not(has_y[d]))
        def _():
            yc[d] = jnp.zeros_like(yc[d])
            for par in range(2):
                yr[par, d] = jnp.zeros_like(yr[par, d])
                ytr[par, d] = jnp.zeros_like(ytr[par, d])

    for i, j in corners:

        @pl.when(jnp.logical_not(has_c[i, j]))
        def _():
            for par in range(2):
                cr[par, i, j] = jnp.zeros_like(cr[par, i, j])

    def remote(src, dst, send, recv, device):
        return pltpu.make_async_remote_copy(
            src_ref=src, dst_ref=dst, send_sem=send, recv_sem=recv,
            device_id=device, device_id_type=MESH,
        )

    def x_copy(par, d):
        return remote(u.at[0, :, pl.ds(4 * d, 4), pl.ds(8, 16)], xr.at[par, 1 - d],
                      xs_sem.at[d], xr_sem.at[par, 1 - d], {"gx": x_of[d]})

    def xt_copy(par, d):
        return remote(t.at[0, :, pl.ds(4 * d, 4)], xtr.at[par, 1 - d],
                      xts_sem.at[d], xtr_sem.at[par, 1 - d], {"gx": x_of[d]})

    def y_copy(par, d):
        return remote(ys.at[d], yr.at[par, 1 - d],
                      ys_sem.at[d], yr_sem.at[par, 1 - d], {"gy": y_of[d]})

    def yt_copy(par, d):
        return remote(yts.at[d], ytr.at[par, 1 - d],
                      yts_sem.at[d], ytr_sem.at[par, 1 - d], {"gy": y_of[d]})

    def corner_copy(par, i, j):
        return remote(ys.at[j, :, pl.ds(4 * i, 4)], cr.at[par, 1 - i, 1 - j],
                      cs_sem.at[i, j], cr_sem.at[par, 1 - i, 1 - j], {"gx": x_of[i], "gy": y_of[j]})

    def xc_copy(d):
        return remote(c.at[:, pl.ds(4 * d, 4)], xc.at[1 - d],
                      xcs_sem.at[d], xcr_sem.at[1 - d], {"gx": x_of[d]})

    def yc_copy(d):
        return remote(ycs.at[d], yc.at[1 - d], ycs_sem.at[d], ycr_sem.at[1 - d], {"gy": y_of[d]})

    def image_copy(slot):
        return remote(u.at[0, 1 - group, :, pl.ds(8, 16)], image_in.at[slot],
                      im_send.at[slot], im_recv.at[slot], partner)

    def start(there, copy):
        @pl.when(there)
        def _():
            copy.start()

    def wait_recv(there, copy):
        @pl.when(there)
        def _():
            copy.wait_recv()

    def wait_send(there, copy):
        @pl.when(there)
        def _():
            copy.wait_send()

    lane = lax.broadcasted_iota(jnp.int32, (16, 128), 1)
    lane4 = lax.broadcasted_iota(jnp.int32, (4, 128), 1)
    lane1 = lax.broadcasted_iota(jnp.int32, (1, 128), 1)
    overwrite = (jnp.logical_and(lane < 4, source_side), jnp.logical_and(lane >= 124, source_side))
    overwrite4 = (jnp.logical_and(lane4 < 4, source_side), jnp.logical_and(lane4 >= 124, source_side))

    for copy in loads:
        copy.wait()

    source_x = source[0] - at_x * 8
    source_y = source[1] - at_y * 16
    inside = (source_x >= 0) & (source_x < 8) & (source_y >= 0) & (source_y < 16)
    source_flat = jnp.where(inside, (source_x * 16 + source_y) * 256 + source[2], -1)
    where_to = jnp.where(source_side, jnp.where(lane1 == 0, source_flat, -1), cell_v[0])
    row_of = jnp.where(where_to < 0, -1, ((where_to >> 7) & 1) * 128 + (where_to >> 8))
    column_of = where_to & 127
    column_hot = jnp.where(
        lax.broadcasted_iota(jnp.int32, (128, 128), 0) == column_of, 1.0, 0.0
    ).astype(BF16)
    row_hot = lax.broadcasted_iota(jnp.int32, (256, 128), 0) == row_of
    layer = lax.broadcasted_iota(jnp.int32, (128, 256), 0) & 7
    depth_of = jnp.where(layer < 4, layer, 248 + layer)
    spread = jnp.where(
        lax.broadcasted_iota(jnp.int32, (128, 256), 1) == depth_of, 1.0, 0.0
    ).astype(BF16)
    own_row = (
        lax.broadcasted_iota(jnp.int32, (8, 16, 128), 2) >> 3
        == lax.broadcasted_iota(jnp.int32, (8, 16, 128), 1)
    )

    def inject(slot, k):
        sample = jnp.where(source_side, jnp.where(lane1 == 0, -wavelet[k], 0.0), trace_v[k, 0])
        total = None
        for part in split3(sample):
            left = jnp.where(row_hot, part, 0.0).astype(BF16)
            total = add(total, lax.dot_general(
                left, column_hot, (((1,), (1,)), ((), ())), preferred_element_type=F32
            ))
        inj[slot] = total.reshape(2, 8, 16, 128)
        total = None
        for part in split3(strip_v[k]):
            left = jnp.where(own_row, part[:, None, :], 0.0).reshape(128, 128).astype(BF16)
            total = add(total, jnp.dot(left, spread, preferred_element_type=F32))
        for h in range(2):
            dense[slot, h] = total[:, 128 * h : 128 * h + 128].reshape(8, 16, 128)

    def own_part(slot, x):
        lower, upper = u[slot, 0, x, 8:24], u[slot, 1, x, 8:24]
        centre = (lower, upper)
        sums = [inj[slot, h, x] + (3.0 * STENCIL[0]) * centre[h] for h in range(2)]
        for k in range(1, 5):
            depth = shifted_sum(lower, upper, k, lane)
            for h in range(2):
                near = depth[h] + (u[slot, h, x, 8 - k : 24 - k] + u[slot, h, x, 8 + k : 24 + k])
                if x - k >= 0:
                    near = near + u[slot, h, x - k, 8:24]
                if x + k < 8:
                    near = near + u[slot, h, x + k, 8:24]
                sums[h] = sums[h] + W[k] * near
        for h in range(2):
            value = 2.0 * centre[h] - u[1 - slot, h, x, 8:24] + cm[h, x] * sums[h]
            value = jnp.where(overwrite[h], dense[slot, h, x], value)
            t[slot, h, x] = value
            if slot == 0:
                yts[0, h, x] = value[0:4]
                yts[1, h, x] = value[12:16]

    def low_rows(ref):
        total = None
        for m in range(4):
            total = add(total, W[4 - m] * ref[m : m + 8])
        return total

    def high_rows(ref):
        total = None
        for m in range(4):
            total = add(total, W[4 - m] * ref[4 - m : 12 - m])
        return total

    def finish(slot, x, planes):
        d = x // 4
        values = []
        for h in range(2):
            extra = None
            for j in range(4):
                distance = x + 4 - j if d == 0 else 8 + j - x
                if distance <= 4:
                    extra = add(extra, W[distance] * planes(h, j))
            low, high = low_rows(yl.at[h, x]), high_rows(yh.at[h, x])
            first = t[slot, h, x, 0:8] + cm[h, x, 0:8] * (extra[0:8] + low)
            second = t[slot, h, x, 8:16] + cm[h, x, 8:16] * (extra[8:16] + high)
            u[1 - slot, h, x, 8:16] = first
            u[1 - slot, h, x, 16:24] = second
            values.append((first, second))
        return values

    def halo(par):
        for i in range(2):
            cl[i, :, :, 0:4] = cr[par, i, 0]
            ch[i, :, :, 8:12] = cr[par, i, 1]
        for d in range(2):
            for h in range(2):
                for j in range(4):
                    extra = None
                    for p in range(8):
                        distance = p + 4 - j if d == 0 else 8 + j - p
                        if distance <= 4:
                            extra = add(extra, W[distance] * u[0, h, p, 8:24])
                    low, high = low_rows(cl.at[d, h, j]), high_rows(ch.at[d, h, j])
                    hx[d, h, j, 0:8] = xcm[d, h, j, 0:8] * (extra[0:8] + low)
                    hx[d, h, j, 8:16] = xcm[d, h, j, 8:16] * (extra[8:16] + high)
        for d in range(2):
            for h in range(2):
                for x in range(8):
                    extra = None
                    for m in range(4):
                        at = 8 - m if d == 0 else 20 + m
                        extra = add(extra, W[4 - m] * u[0, h, x, at : at + 4])
                    i = x // 4
                    for j in range(4):
                        distance = x + 4 - j if i == 0 else 8 + j - x
                        if distance <= 4:
                            extra = extra + W[distance] * cr[par, i, d, h, j]
                    hy[d, h, x] = ycm[d, h, x] * extra

    def send_t(par):
        for d in range(2):
            for x in range(4 * d, 4 * d + 4):
                own_part(0, x)
            if par is not None:
                start(has_x[d], xt_copy(par, d))
        if par is not None:
            for d in range(2):
                start(has_y[d], yt_copy(par, d))

    for h in range(2):
        cm[h] = jnp.where(overwrite[h], 0.0, c[h])
    for d in range(2):
        ys[d] = u[0, :, :, 8 + 12 * d : 12 + 12 * d]
        ycs[d] = c[:, :, 12 * d : 12 * d + 4]
    inject(0, 0)
    send_t(None)

    pl.semaphore_wait(barrier, count)
    for d in range(2):
        start(has_x[d], x_copy(0, d))
    for d in range(2):
        start(has_y[d], y_copy(0, d))
    for i, j in corners:
        start(has_c[i, j], corner_copy(0, i, j))
    for d in range(2):
        start(has_x[d], xc_copy(d))
    for d in range(2):
        start(has_y[d], yc_copy(d))
    for d in range(2):
        start(has_x[d], xt_copy(0, d))
    for d in range(2):
        start(has_y[d], yt_copy(0, d))

    def one_round(half, par):
        first, final = half == 0, half == 1
        more = True if par == 0 else first
        step = 4 * half + 2 * par
        inject(1, step + 1)
        if par == 0:
            inject(0, step + 2)

            @pl.when(final)
            def _():
                image_copy(0).wait()
                image[...] = u[0, group, :, 8:24] * image_in[0]

        else:

            @pl.when(more)
            def _():
                inject(0, step + 2)

        for d in range(2):
            wait_recv(has_y[d], y_copy(par, 1 - d))
        for x in range(8):
            yl[:, x, 0:4] = yr[par, 0, :, x]
            yh[:, x, 8:12] = yr[par, 1, :, x]
        for d in range(2):
            wait_recv(has_x[d], x_copy(par, 1 - d))
            for x in range(4 * d, 4 * d + 4):
                finish(0, x, lambda h, j: xr[par, d, h, j])

        for x in range(8):
            own_part(1, x)
        if par == 0:

            @pl.when(first)
            def _():
                for d in range(2):
                    wait_recv(has_x[d], xc_copy(1 - d))
                    wait_recv(has_y[d], yc_copy(1 - d))
                    for h in range(2):
                        xcm[d, h] = jnp.where(overwrite[h], 0.0, xc[d, h])
                        ycm[d, h] = jnp.where(overwrite4[h], 0.0, yc[d, h])
                for d in range(2):
                    wait_send(has_x[d], xc_copy(d))
                    wait_send(has_y[d], yc_copy(d))

        else:

            @pl.when(final)
            def _():
                for h in range(2):
                    later_out[0, :, :, 128 * h : 128 * h + 128] = u[1, h, :, 8:24]

        for i, j in corners:
            wait_recv(has_c[i, j], corner_copy(par, 1 - i, 1 - j))
        halo(par)
        for d in range(2):
            wait_send(has_x[d], x_copy(par, d))
            wait_send(has_y[d], y_copy(par, d))
        for i, j in corners:
            wait_send(has_c[i, j], corner_copy(par, i, j))
        for d in range(2):
            wait_recv(has_y[d], yt_copy(par, 1 - d))
        for x in range(8):
            for h in range(2):
                yl[h, x, 0:4] = ytr[par, 0, h, x] + hy[0, h, x]
                yh[h, x, 8:12] = ytr[par, 1, h, x] + hy[1, h, x]
        for d in range(2):
            wait_recv(has_x[d], xt_copy(par, 1 - d))
            for h in range(2):
                for j in range(4):
                    hx[d, h, j] = hx[d, h, j] + xtr[par, d, h, j]
            for x in range(4 * d, 4 * d + 4):
                values = finish(1, x, lambda h, j: hx[d, h, j])
                for h in range(2):
                    ys[0, h, x] = values[h][0][0:4]
                    ys[1, h, x] = values[h][1][4:8]
            start(jnp.logical_and(more, has_x[d]), x_copy(1 - par, d))
        for d in range(2):
            start(jnp.logical_and(more, has_y[d]), y_copy(1 - par, d))
        for i, j in corners:
            start(jnp.logical_and(more, has_c[i, j]), corner_copy(1 - par, i, j))
        for d in range(2):
            wait_send(has_x[d], xt_copy(par, d))
            wait_send(has_y[d], yt_copy(par, d))
        if par == 0:
            send_t(1 - par)
        else:

            @pl.when(first)
            def _():
                image_copy(0).start()
                send_t(1 - par)

            @pl.when(final)
            def _():
                image_copy(1).start()

    def two_rounds(half, carry):
        one_round(half, 0)
        one_round(half, 1)
        return carry

    lax.fori_loop(0, 2, two_rounds, 0)
    for h in range(2):
        now_out[0, :, :, 128 * h : 128 * h + 128] = u[0, h, :, 8:24]
    image_copy(1).wait()
    image_out[...] = image[...] + u[0, group, :, 8:24] * image_in[1]


def local(state_now, state_later, courant, strips, traces, receiver_cells, source_point, wavelet):
    any_space = pl.BlockSpec(memory_space=pl.ANY)
    vmem = pl.BlockSpec(memory_space=pltpu.VMEM)
    dma = pltpu.SemaphoreType.DMA
    v = pltpu.VMEM
    return pl.pallas_call(
        kernel,
        out_shape=(
            jax.ShapeDtypeStruct((8, 16, 128), F32),
            jax.ShapeDtypeStruct((1, 8, 16, 256), F32),
            jax.ShapeDtypeStruct((1, 8, 16, 256), F32),
        ),
        in_specs=[any_space] * 8,
        out_specs=(vmem,) * 3,
        scratch_shapes=[
            v((2, 2, 8, 32, 128), F32),
            v((2, 2, 8, 16, 128), F32),
            v((2, 8, 16, 128), F32),
            v((2, 8, 16, 128), F32),
            v((2, 2, 2, 4, 16, 128), F32),
            v((2, 2, 2, 4, 16, 128), F32),
            v((2, 2, 2, 8, 4, 128), F32),
            v((2, 2, 2, 8, 4, 128), F32),
            v((2, 2, 2, 2, 4, 4, 128), F32),
            v((2, 2, 4, 16, 128), F32),
            v((2, 2, 8, 4, 128), F32),
            v((2, 2, 4, 16, 128), F32),
            v((2, 2, 8, 4, 128), F32),
            v((2, 2, 8, 4, 128), F32),
            v((2, 2, 8, 4, 128), F32),
            v((2, 2, 8, 4, 128), F32),
            v((2, 8, 16, 128), F32),
            v((2, 8, 16, 128), F32),
            v((2, 2, 4, 16, 128), F32),
            v((2, 2, 4, 16, 128), F32),
            v((2, 2, 4, 16, 128), F32),
            v((2, 2, 8, 4, 128), F32),
            v((2, 2, 8, 16, 128), F32),
            v((2, 2, 8, 16, 128), F32),
            v((2, 8, 16, 128), F32),
            v((8, 16, 128), F32),
            v((8, 8, 128), F32),
            v((8, 1, 1, 128), F32),
            v((1, 1, 128), jnp.int32),
            pltpu.SMEM((3,), jnp.int32),
            pltpu.SMEM((8,), F32),
            dma((11,)),
            dma((2,)), dma((2,)), dma((2,)), dma((2,)), dma((2, 2)), dma((2,)), dma((2,)),
            dma((2, 2)), dma((2, 2)), dma((2, 2)), dma((2, 2)), dma((2, 2, 2)), dma((2,)), dma((2,)),
            dma((2,)), dma((2,)),
        ],
        compiler_params=pltpu.CompilerParams(collective_id=0, has_side_effects=True),
    )(state_now, state_later, courant, strips, traces, receiver_cells, source_point, wavelet)


def solution(mesh):
    in_specs = (
        P("grp", "gx", "gy", None),
        P("grp", "gx", "gy", None),
        P("gx", "gy", None),
        P(None, "gx", "gy"),
        P(None, "gx", "gy", None),
        P("gx", "gy", None),
        P(),
        P(),
    )
    out_specs = (P("gx", "gy", "grp"), P("grp", "gx", "gy", None), P("grp", "gx", "gy", None))
    return jax.shard_map(local, mesh=mesh, in_specs=in_specs, out_specs=out_specs, check_vma=False)
```

```python
import jax
import jax.numpy as jnp
from jax import lax
from jax.experimental import pallas as pl
from jax.experimental.pallas import tpu as pltpu
from jax.sharding import PartitionSpec as P

STENCIL = (-205.0 / 72.0, 8.0 / 5.0, -1.0 / 5.0, 8.0 / 315.0, -1.0 / 560.0)
W = (None,) + STENCIL[1:]
MESH = pl.DeviceIdType.MESH
F32 = jnp.float32
BF16 = jnp.bfloat16


def split3(value):
    high = value.astype(BF16).astype(F32)
    rest = value - high
    middle = rest.astype(BF16).astype(F32)
    return high, middle, rest - middle


def shifted_sum(lower, upper, k, lane):
    lower_up, upper_up = pltpu.roll(lower, k, 1), pltpu.roll(upper, k, 1)
    lower_down, upper_down = pltpu.roll(lower, 128 - k, 1), pltpu.roll(upper, 128 - k, 1)
    zero = jnp.zeros_like(lower)
    first, last = lane >= k, lane < 128 - k
    return (
        jnp.where(first, lower_up, zero) + jnp.where(last, lower_down, upper_down),
        jnp.where(first, upper_up, lower_up) + jnp.where(last, upper_down, zero),
    )


def add(total, term):
    return term if total is None else total + term


def kernel(
    now, later, courant, strips, traces, cells, source_in, wavelet_in,
    image_out, now_out, later_out,
    u, t, c, cm, xr, xtr, yr, ytr, cr, xc, yc, xcm, ycm, ys, yts, ycs,
    yl, yh, cl, ch, hx, hy, inj, dense, image_in, image,
    strip_v, trace_v, cell_v, source, wavelet,
    load_sem, xs_sem, xts_sem, ys_sem, yts_sem, cs_sem, xcs_sem, ycs_sem,
    xr_sem, xtr_sem, yr_sem, ytr_sem, cr_sem, xcr_sem, ycr_sem, im_send, im_recv, ready,
):
    group = lax.axis_index("grp")
    at_x = lax.axis_index("gx")
    at_y = lax.axis_index("gy")
    size_x = lax.axis_size("gx")
    size_y = lax.axis_size("gy")
    source_side = group == 0
    has_x = (at_x > 0, at_x < size_x - 1)
    has_y = (at_y > 0, at_y < size_y - 1)
    x_of = (at_x - 1, at_x + 1)
    y_of = (at_y - 1, at_y + 1)
    partner = {"grp": 1 - group}
    corners = [(i, j) for i in range(2) for j in range(2)]
    has_c = {(i, j): jnp.logical_and(has_x[i], has_y[j]) for i, j in corners}

    barrier = pltpu.get_barrier_semaphore()
    count = jnp.int32(1)
    others = [(has_x[d], {"gx": x_of[d]}) for d in range(2)]
    others += [(has_y[d], {"gy": y_of[d]}) for d in range(2)]
    pl.semaphore_signal(barrier, inc=1, device_id=partner, device_id_type=MESH)
    for there, device in others:
        count = count + there.astype(jnp.int32)

        @pl.when(there)
        def _():
            pl.semaphore_signal(barrier, inc=1, device_id=device, device_id_type=MESH)

    loads = []
    for h in range(2):
        zs = pl.ds(128 * h, 128)
        loads.append((now.at[0, :, :, zs], u.at[0, h, :, pl.ds(8, 16)]))
        loads.append((later.at[0, :, :, zs], u.at[1, h, :, pl.ds(8, 16)]))
        loads.append((courant.at[:, :, zs], c.at[h]))
    loads += [(cells, cell_v), (traces, trace_v), (strips, strip_v)]
    loads += [(source_in, source), (wavelet_in, wavelet)]
    loads = [pltpu.make_async_copy(a, b, load_sem.at[i]) for i, (a, b) in enumerate(loads)]
    for copy in loads:
        copy.start()

    for slot in range(2):
        u[slot, :, :, 0:8] = jnp.zeros((2, 8, 8, 128), F32)
        u[slot, :, :, 24:32] = jnp.zeros((2, 8, 8, 128), F32)
    for ref in (yl, yh, cl, ch):
        ref[...] = jnp.zeros_like(ref)
    for d in range(2):

        @pl.when(jnp.logical_not(has_x[d]))
        def _():
            xc[d] = jnp.zeros_like(xc[d])
            for par in range(2):
                xr[par, d] = jnp.zeros_like(xr[par, d])
                xtr[par, d] = jnp.zeros_like(xtr[par, d])

        @pl.when(jnp.logical_not(has_y[d]))
        def _():
            yc[d] = jnp.zeros_like(yc[d])
            for par in range(2):
                yr[par, d] = jnp.zeros_like(yr[par, d])
                ytr[par, d] = jnp.zeros_like(ytr[par, d])

    for i, j in corners:

        @pl.when(jnp.logical_not(has_c[i, j]))
        def _():
            for par in range(2):
                cr[par, i, j] = jnp.zeros_like(cr[par, i, j])

    def remote(src, dst, send, recv, device):
        return pltpu.make_async_remote_copy(
            src_ref=src, dst_ref=dst, send_sem=send, recv_sem=recv,
            device_id=device, device_id_type=MESH,
        )

    def x_copy(par, d):
        return remote(u.at[0, :, pl.ds(4 * d, 4), pl.ds(8, 16)], xr.at[par, 1 - d],
                      xs_sem.at[d], xr_sem.at[par, 1 - d], {"gx": x_of[d]})

    def xt_copy(par, d):
        return remote(t.at[0, :, pl.ds(4 * d, 4)], xtr.at[par, 1 - d],
                      xts_sem.at[d], xtr_sem.at[par, 1 - d], {"gx": x_of[d]})

    def y_copy(par, d):
        return remote(ys.at[d], yr.at[par, 1 - d],
                      ys_sem.at[d], yr_sem.at[par, 1 - d], {"gy": y_of[d]})

    def yt_copy(par, d):
        return remote(yts.at[d], ytr.at[par, 1 - d],
                      yts_sem.at[d], ytr_sem.at[par, 1 - d], {"gy": y_of[d]})

    def corner_copy(par, i, j):
        return remote(ys.at[j, :, pl.ds(4 * i, 4)], cr.at[par, 1 - i, 1 - j],
                      cs_sem.at[i, j], cr_sem.at[par, 1 - i, 1 - j], {"gx": x_of[i], "gy": y_of[j]})

    def xc_copy(d):
        return remote(c.at[:, pl.ds(4 * d, 4)], xc.at[1 - d],
                      xcs_sem.at[d], xcr_sem.at[1 - d], {"gx": x_of[d]})

    def yc_copy(d):
        return remote(ycs.at[d], yc.at[1 - d], ycs_sem.at[d], ycr_sem.at[1 - d], {"gy": y_of[d]})

    def image_copy(slot):
        return remote(u.at[0, 1 - group, :, pl.ds(8, 16)], image_in.at[slot],
                      im_send.at[slot], im_recv.at[slot], partner)

    def start(there, copy):
        @pl.when(there)
        def _():
            copy.start()

    def wait_recv(there, copy):
        @pl.when(there)
        def _():
            copy.wait_recv()

    def wait_send(there, copy):
        @pl.when(there)
        def _():
            copy.wait_send()

    lane = lax.broadcasted_iota(jnp.int32, (16, 128), 1)
    lane4 = lax.broadcasted_iota(jnp.int32, (4, 128), 1)
    lane1 = lax.broadcasted_iota(jnp.int32, (1, 128), 1)
    overwrite = (jnp.logical_and(lane < 4, source_side), jnp.logical_and(lane >= 124, source_side))
    overwrite4 = (jnp.logical_and(lane4 < 4, source_side), jnp.logical_and(lane4 >= 124, source_side))

    for copy in loads:
        copy.wait()

    source_x = source[0] - at_x * 8
    source_y = source[1] - at_y * 16
    inside = (source_x >= 0) & (source_x < 8) & (source_y >= 0) & (source_y < 16)
    source_flat = jnp.where(inside, (source_x * 16 + source_y) * 256 + source[2], -1)
    where_to = jnp.where(source_side, jnp.where(lane1 == 0, source_flat, -1), cell_v[0])
    row_of = jnp.where(where_to < 0, -1, ((where_to >> 7) & 1) * 128 + (where_to >> 8))
    column_of = where_to & 127
    column_hot = jnp.where(
        lax.broadcasted_iota(jnp.int32, (128, 128), 0) == column_of, 1.0, 0.0
    ).astype(BF16)
    row_hot = lax.broadcasted_iota(jnp.int32, (256, 128), 0) == row_of
    layer = lax.broadcasted_iota(jnp.int32, (128, 256), 0) & 7
    depth_of = jnp.where(layer < 4, layer, 248 + layer)
    spread = jnp.where(
        lax.broadcasted_iota(jnp.int32, (128, 256), 1) == depth_of, 1.0, 0.0
    ).astype(BF16)
    own_row = (
        lax.broadcasted_iota(jnp.int32, (8, 16, 128), 2) >> 3
        == lax.broadcasted_iota(jnp.int32, (8, 16, 128), 1)
    )

    def inject(slot, k):
        sample = jnp.where(source_side, jnp.where(lane1 == 0, -wavelet[k], 0.0), trace_v[k, 0])
        total = None
        for part in split3(sample):
            left = jnp.where(row_hot, part, 0.0).astype(BF16)
            total = add(total, lax.dot_general(
                left, column_hot, (((1,), (1,)), ((), ())), preferred_element_type=F32
            ))
        inj[slot] = total.reshape(2, 8, 16, 128)
        total = None
        for part in split3(strip_v[k]):
            left = jnp.where(own_row, part[:, None, :], 0.0).reshape(128, 128).astype(BF16)
            total = add(total, jnp.dot(left, spread, preferred_element_type=F32))
        for h in range(2):
            dense[slot, h] = total[:, 128 * h : 128 * h + 128].reshape(8, 16, 128)

    def own_part(slot, x):
        lower, upper = u[slot, 0, x, 8:24], u[slot, 1, x, 8:24]
        centre = (lower, upper)
        sums = [inj[slot, h, x] + (3.0 * STENCIL[0]) * centre[h] for h in range(2)]
        for k in range(1, 5):
            depth = shifted_sum(lower, upper, k, lane)
            for h in range(2):
                near = depth[h] + (u[slot, h, x, 8 - k : 24 - k] + u[slot, h, x, 8 + k : 24 + k])
                if x - k >= 0:
                    near = near + u[slot, h, x - k, 8:24]
                if x + k < 8:
                    near = near + u[slot, h, x + k, 8:24]
                sums[h] = sums[h] + W[k] * near
        for h in range(2):
            value = 2.0 * centre[h] - u[1 - slot, h, x, 8:24] + cm[h, x] * sums[h]
            value = jnp.where(overwrite[h], dense[slot, h, x], value)
            t[slot, h, x] = value
            if slot == 0:
                yts[0, h, x] = value[0:4]
                yts[1, h, x] = value[12:16]

    def low_rows(ref):
        total = None
        for m in range(4):
            total = add(total, W[4 - m] * ref[m : m + 8])
        return total

    def high_rows(ref):
        total = None
        for m in range(4):
            total = add(total, W[4 - m] * ref[4 - m : 12 - m])
        return total

    def finish(slot, x, planes):
        d = x // 4
        values = []
        for h in range(2):
            extra = None
            for j in range(4):
                distance = x + 4 - j if d == 0 else 8 + j - x
                if distance <= 4:
                    extra = add(extra, W[distance] * planes(h, j))
            low, high = low_rows(yl.at[h, x]), high_rows(yh.at[h, x])
            first = t[slot, h, x, 0:8] + cm[h, x, 0:8] * (extra[0:8] + low)
            second = t[slot, h, x, 8:16] + cm[h, x, 8:16] * (extra[8:16] + high)
            u[1 - slot, h, x, 8:16] = first
            u[1 - slot, h, x, 16:24] = second
            values.append((first, second))
        return values

    def halo_cross():
        for d in range(2):
            for h in range(2):
                for j in range(4):
                    extra = None
                    for p in range(8):
                        distance = p + 4 - j if d == 0 else 8 + j - p
                        if distance <= 4:
                            extra = add(extra, W[distance] * u[0, h, p, 8:24])
                    hx[d, h, j] = extra
                for x in range(8):
                    extra = None
                    for m in range(4):
                        at = 8 - m if d == 0 else 20 + m
                        extra = add(extra, W[4 - m] * u[0, h, x, at : at + 4])
                    hy[d, h, x] = extra

    def halo_corners(par, i):
        cl[i, :, :, 0:4] = cr[par, i, 0]
        ch[i, :, :, 8:12] = cr[par, i, 1]
        for h in range(2):
            for j in range(4):
                low, high = low_rows(cl.at[i, h, j]), high_rows(ch.at[i, h, j])
                for rows, extra in ((slice(0, 8), low), (slice(8, 16), high)):
                    hx[i, h, j, rows] = xtr[par, i, h, j, rows] + xcm[i, h, j, rows] * (hx[i, h, j, rows] + extra)
            for x in range(4 * i, 4 * i + 4):
                for d in range(2):
                    extra = hy[d, h, x]
                    for j in range(4):
                        distance = x + 4 - j if i == 0 else 8 + j - x
                        if distance <= 4:
                            extra = extra + W[distance] * cr[par, i, d, h, j]
                    value = ytr[par, d, h, x] + ycm[d, h, x] * extra
                    if d == 0:
                        yl[h, x, 0:4] = value
                    else:
                        yh[h, x, 8:12] = value

    def send_t(par):
        for d in range(2):
            for x in range(4 * d, 4 * d + 4):
                own_part(0, x)
            if par is not None:
                start(has_x[d], xt_copy(par, d))
        if par is not None:
            for d in range(2):
                start(has_y[d], yt_copy(par, d))

    for h in range(2):
        cm[h] = jnp.where(overwrite[h], 0.0, c[h])
    for d in range(2):
        ys[d] = u[0, :, :, 8 + 12 * d : 12 + 12 * d]
        ycs[d] = c[:, :, 12 * d : 12 * d + 4]
    inject(0, 0)
    send_t(None)

    pl.semaphore_wait(barrier, count)
    for d in range(2):
        start(has_x[d], x_copy(0, d))
    for d in range(2):
        start(has_y[d], y_copy(0, d))
    for d in range(2):

        @pl.when(has_y[d])
        def _():
            pl.semaphore_signal(ready.at[1 - d], inc=1, device_id={"gy": y_of[d]}, device_id_type=MESH)

    for d in range(2):
        start(has_x[d], xt_copy(0, d))
    for d in range(2):
        start(has_y[d], yt_copy(0, d))
    for j in range(2):

        @pl.when(has_y[j])
        def _():
            pl.semaphore_wait(ready.at[j], 1)

        for i in range(2):
            start(has_c[i, j], corner_copy(0, i, j))
    for d in range(2):
        start(has_x[d], xc_copy(d))
    for d in range(2):
        start(has_y[d], yc_copy(d))

    def one_round(half, par):
        first, final = half == 0, half == 1
        more = True if par == 0 else first
        step = 4 * half + 2 * par
        inject(1, step + 1)
        if par == 0:
            inject(0, step + 2)

            @pl.when(final)
            def _():
                image_copy(0).wait()
                image[...] = u[0, group, :, 8:24] * image_in[0]

        else:

            @pl.when(more)
            def _():
                inject(0, step + 2)

        for d in range(2):
            wait_recv(has_y[d], y_copy(par, 1 - d))
        for x in range(8):
            yl[:, x, 0:4] = yr[par, 0, :, x]
            yh[:, x, 8:12] = yr[par, 1, :, x]
        for d in range(2):
            wait_recv(has_x[d], x_copy(par, 1 - d))
            for x in range(4 * d, 4 * d + 4):
                finish(0, x, lambda h, j: xr[par, d, h, j])

        for x in range(8):
            own_part(1, x)
        halo_cross()
        if par == 0:

            @pl.when(first)
            def _():
                for d in range(2):
                    wait_recv(has_x[d], xc_copy(1 - d))
                    wait_recv(has_y[d], yc_copy(1 - d))
                    for h in range(2):
                        xcm[d, h] = jnp.where(overwrite[h], 0.0, xc[d, h])
                        ycm[d, h] = jnp.where(overwrite4[h], 0.0, yc[d, h])
                for d in range(2):
                    wait_send(has_x[d], xc_copy(d))
                    wait_send(has_y[d], yc_copy(d))

        else:

            @pl.when(final)
            def _():
                for h in range(2):
                    later_out[0, :, :, 128 * h : 128 * h + 128] = u[1, h, :, 8:24]

        for d in range(2):
            wait_send(has_x[d], x_copy(par, d))
            wait_send(has_y[d], y_copy(par, d))
        for i, j in corners:
            wait_send(has_c[i, j], corner_copy(par, i, j))
        for d in range(2):
            wait_recv(has_y[d], yt_copy(par, 1 - d))
        for d in range(2):
            for j in range(2):
                wait_recv(has_c[d, j], corner_copy(par, 1 - d, 1 - j))
            wait_recv(has_x[d], xt_copy(par, 1 - d))
            halo_corners(par, d)
            for x in range(4 * d, 4 * d + 4):
                values = finish(1, x, lambda h, j: hx[d, h, j])
                for h in range(2):
                    ys[0, h, x] = values[h][0][0:4]
                    ys[1, h, x] = values[h][1][4:8]
            for j in range(2):
                start(jnp.logical_and(more, has_c[d, j]), corner_copy(1 - par, d, j))
            start(jnp.logical_and(more, has_x[d]), x_copy(1 - par, d))
        for d in range(2):
            start(jnp.logical_and(more, has_y[d]), y_copy(1 - par, d))
        for d in range(2):
            wait_send(has_x[d], xt_copy(par, d))
            wait_send(has_y[d], yt_copy(par, d))
        if par == 0:
            send_t(1 - par)
        else:

            @pl.when(first)
            def _():
                image_copy(0).start()
                send_t(1 - par)

            @pl.when(final)
            def _():
                image_copy(1).start()

    def two_rounds(half, carry):
        one_round(half, 0)
        one_round(half, 1)
        return carry

    lax.fori_loop(0, 2, two_rounds, 0)
    for h in range(2):
        now_out[0, :, :, 128 * h : 128 * h + 128] = u[0, h, :, 8:24]
    image_copy(1).wait()
    image_out[...] = image[...] + u[0, group, :, 8:24] * image_in[1]


def local(state_now, state_later, courant, strips, traces, receiver_cells, source_point, wavelet):
    any_space = pl.BlockSpec(memory_space=pl.ANY)
    vmem = pl.BlockSpec(memory_space=pltpu.VMEM)
    dma = pltpu.SemaphoreType.DMA
    v = pltpu.VMEM
    return pl.pallas_call(
        kernel,
        out_shape=(
            v((8, 16, 128), F32),
            v((1, 8, 16, 256), F32),
            v((1, 8, 16, 256), F32),
        ),
        in_specs=[any_space] * 8,
        out_specs=(vmem,) * 3,
        scratch_shapes=[
            v((2, 2, 8, 32, 128), F32),
            v((2, 2, 8, 16, 128), F32),
            v((2, 8, 16, 128), F32),
            v((2, 8, 16, 128), F32),
            v((2, 2, 2, 4, 16, 128), F32),
            v((2, 2, 2, 4, 16, 128), F32),
            v((2, 2, 2, 8, 4, 128), F32),
            v((2, 2, 2, 8, 4, 128), F32),
            v((2, 2, 2, 2, 4, 4, 128), F32),
            v((2, 2, 4, 16, 128), F32),
            v((2, 2, 8, 4, 128), F32),
            v((2, 2, 4, 16, 128), F32),
            v((2, 2, 8, 4, 128), F32),
            v((2, 2, 8, 4, 128), F32),
            v((2, 2, 8, 4, 128), F32),
            v((2, 2, 8, 4, 128), F32),
            v((2, 8, 16, 128), F32),
            v((2, 8, 16, 128), F32),
            v((2, 2, 4, 16, 128), F32),
            v((2, 2, 4, 16, 128), F32),
            v((2, 2, 4, 16, 128), F32),
            v((2, 2, 8, 4, 128), F32),
            v((2, 2, 8, 16, 128), F32),
            v((2, 2, 8, 16, 128), F32),
            v((2, 8, 16, 128), F32),
            v((8, 16, 128), F32),
            v((8, 8, 128), F32),
            v((8, 1, 1, 128), F32),
            v((1, 1, 128), jnp.int32),
            pltpu.SMEM((3,), jnp.int32),
            pltpu.SMEM((8,), F32),
            dma((11,)),
            dma((2,)), dma((2,)), dma((2,)), dma((2,)), dma((2, 2)), dma((2,)), dma((2,)),
            dma((2, 2)), dma((2, 2)), dma((2, 2)), dma((2, 2)), dma((2, 2, 2)), dma((2,)), dma((2,)),
            dma((2,)), dma((2,)),
            pltpu.SemaphoreType.REGULAR((2,)),
        ],
        compiler_params=pltpu.CompilerParams(collective_id=0, has_side_effects=True),
    )(state_now, state_later, courant, strips, traces, receiver_cells, source_point, wavelet)


def solution(mesh):
    in_specs = (
        P("grp", "gx", "gy", None),
        P("grp", "gx", "gy", None),
        P("gx", "gy", None),
        P(None, "gx", "gy"),
        P(None, "gx", "gy", None),
        P("gx", "gy", None),
        P(),
        P(),
    )
    out_specs = (P("gx", "gy", "grp"), P("grp", "gx", "gy", None), P("grp", "gx", "gy", None))
    return jax.shard_map(local, mesh=mesh, in_specs=in_specs, out_specs=out_specs, check_vma=False)
```

```python
import jax
import jax.numpy as jnp
from jax import lax
from jax.experimental import pallas as pl
from jax.experimental.pallas import tpu as pltpu
from jax.sharding import PartitionSpec as P

STENCIL = (-205.0 / 72.0, 8.0 / 5.0, -1.0 / 5.0, 8.0 / 315.0, -1.0 / 560.0)
W = (None,) + STENCIL[1:]
MESH = pl.DeviceIdType.MESH
F32 = jnp.float32
BF16 = jnp.bfloat16


def split3(value):
    high = value.astype(BF16).astype(F32)
    rest = value - high
    middle = rest.astype(BF16).astype(F32)
    return high, middle, rest - middle


def shifted_sum(lower, upper, k, lane):
    lower_up, upper_up = pltpu.roll(lower, k, 1), pltpu.roll(upper, k, 1)
    lower_down, upper_down = pltpu.roll(lower, 128 - k, 1), pltpu.roll(upper, 128 - k, 1)
    zero = jnp.zeros_like(lower)
    first, last = lane >= k, lane < 128 - k
    return (
        jnp.where(first, lower_up, zero) + jnp.where(last, lower_down, upper_down),
        jnp.where(first, upper_up, lower_up) + jnp.where(last, upper_down, zero),
    )


def add(total, term):
    return term if total is None else total + term


def kernel(
    now, later, courant, strips, traces, cells, source_in, wavelet_in,
    image_out, now_out, later_out,
    u, t, c, cm, xr, xtr, yr, ytr, cr, xc, yc, xcm, ycm, ys, yts, ycs,
    yl, yh, cl, ch, hx, hy, inj, dense, image_in, image,
    strip_v, trace_v, cell_v, source, wavelet,
    load_sem, xs_sem, xts_sem, ys_sem, yts_sem, cs_sem, xcs_sem, ycs_sem,
    xr_sem, xtr_sem, yr_sem, ytr_sem, cr_sem, xcr_sem, ycr_sem, im_send, im_recv, ready,
):
    group = lax.axis_index("grp")
    at_x = lax.axis_index("gx")
    at_y = lax.axis_index("gy")
    size_x = lax.axis_size("gx")
    size_y = lax.axis_size("gy")
    source_side = group == 0
    has_x = (at_x > 0, at_x < size_x - 1)
    has_y = (at_y > 0, at_y < size_y - 1)
    x_of = (at_x - 1, at_x + 1)
    y_of = (at_y - 1, at_y + 1)
    partner = {"grp": 1 - group}
    corners = [(i, j) for i in range(2) for j in range(2)]
    has_c = {(i, j): jnp.logical_and(has_x[i], has_y[j]) for i, j in corners}

    barrier = pltpu.get_barrier_semaphore()
    count = jnp.int32(1)
    others = [(has_x[d], {"gx": x_of[d]}) for d in range(2)]
    others += [(has_y[d], {"gy": y_of[d]}) for d in range(2)]
    pl.semaphore_signal(barrier, inc=1, device_id=partner, device_id_type=MESH)
    for there, device in others:
        count = count + there.astype(jnp.int32)

        @pl.when(there)
        def _():
            pl.semaphore_signal(barrier, inc=1, device_id=device, device_id_type=MESH)

    loads = []
    for h in range(2):
        zs = pl.ds(128 * h, 128)
        loads.append((now.at[0, :, :, zs], u.at[0, h, :, pl.ds(8, 16)]))
        loads.append((later.at[0, :, :, zs], u.at[1, h, :, pl.ds(8, 16)]))
        loads.append((courant.at[:, :, zs], c.at[h]))
    loads += [(cells, cell_v), (traces, trace_v), (strips, strip_v)]
    loads += [(source_in, source), (wavelet_in, wavelet)]
    loads = [pltpu.make_async_copy(a, b, load_sem.at[i]) for i, (a, b) in enumerate(loads)]
    for copy in loads:
        copy.start()

    def remote(src, dst, send, recv, device):
        return pltpu.make_async_remote_copy(
            src_ref=src, dst_ref=dst, send_sem=send, recv_sem=recv,
            device_id=device, device_id_type=MESH,
        )

    def x_copy(par, d):
        return remote(u.at[0, :, pl.ds(4 * d, 4), pl.ds(8, 16)], xr.at[par, 1 - d],
                      xs_sem.at[d], xr_sem.at[par, 1 - d], {"gx": x_of[d]})

    def xt_copy(par, d):
        return remote(t.at[0, :, pl.ds(4 * d, 4)], xtr.at[par, 1 - d],
                      xts_sem.at[d], xtr_sem.at[par, 1 - d], {"gx": x_of[d]})

    def y_copy(par, d):
        return remote(ys.at[d], yr.at[par, 1 - d],
                      ys_sem.at[d], yr_sem.at[par, 1 - d], {"gy": y_of[d]})

    def yt_copy(par, d):
        return remote(yts.at[d], ytr.at[par, 1 - d],
                      yts_sem.at[d], ytr_sem.at[par, 1 - d], {"gy": y_of[d]})

    def corner_copy(par, i, j):
        return remote(ys.at[j, :, pl.ds(4 * i, 4)], cr.at[par, 1 - i, 1 - j],
                      cs_sem.at[i, j], cr_sem.at[par, 1 - i, 1 - j], {"gx": x_of[i], "gy": y_of[j]})

    def xc_copy(d):
        return remote(c.at[:, pl.ds(4 * d, 4)], xc.at[1 - d],
                      xcs_sem.at[d], xcr_sem.at[1 - d], {"gx": x_of[d]})

    def x_first(d, h):
        return remote(now.at[0, pl.ds(4 * d, 4), :, pl.ds(128 * h, 128)], xr.at[0, 1 - d, h],
                      xs_sem.at[d], xr_sem.at[0, 1 - d], {"gx": x_of[d]})

    def xc_first(d, h):
        return remote(courant.at[pl.ds(4 * d, 4), :, pl.ds(128 * h, 128)], xc.at[1 - d, h],
                      xcs_sem.at[d], xcr_sem.at[1 - d], {"gx": x_of[d]})

    def yc_copy(d):
        return remote(ycs.at[d], yc.at[1 - d], ycs_sem.at[d], ycr_sem.at[1 - d], {"gy": y_of[d]})

    def image_copy(slot):
        return remote(u.at[0, 1 - group, :, pl.ds(8, 16)], image_in.at[slot],
                      im_send.at[slot], im_recv.at[slot], partner)

    def start(there, copy):
        @pl.when(there)
        def _():
            copy.start()

    def wait_recv(there, copy):
        @pl.when(there)
        def _():
            copy.wait_recv()

    def wait_send(there, copy):
        @pl.when(there)
        def _():
            copy.wait_send()

    pl.semaphore_wait(barrier, count)
    for d in range(2):
        for h in range(2):
            start(has_x[d], x_first(d, h))
    for d in range(2):

        @pl.when(has_y[d])
        def _():
            pl.semaphore_signal(ready.at[1 - d], inc=1, device_id={"gy": y_of[d]}, device_id_type=MESH)

    for d in range(2):
        for h in range(2):
            start(has_x[d], xc_first(d, h))

    for slot in range(2):
        u[slot, :, :, 0:8] = jnp.zeros((2, 8, 8, 128), F32)
        u[slot, :, :, 24:32] = jnp.zeros((2, 8, 8, 128), F32)
    for ref in (yl, yh, cl, ch):
        ref[...] = jnp.zeros_like(ref)
    for d in range(2):

        @pl.when(jnp.logical_not(has_x[d]))
        def _():
            xc[d] = jnp.zeros_like(xc[d])
            for par in range(2):
                xr[par, d] = jnp.zeros_like(xr[par, d])
                xtr[par, d] = jnp.zeros_like(xtr[par, d])

        @pl.when(jnp.logical_not(has_y[d]))
        def _():
            yc[d] = jnp.zeros_like(yc[d])
            for par in range(2):
                yr[par, d] = jnp.zeros_like(yr[par, d])
                ytr[par, d] = jnp.zeros_like(ytr[par, d])

    for i, j in corners:

        @pl.when(jnp.logical_not(has_c[i, j]))
        def _():
            for par in range(2):
                cr[par, i, j] = jnp.zeros_like(cr[par, i, j])

    lane = lax.broadcasted_iota(jnp.int32, (16, 128), 1)
    lane4 = lax.broadcasted_iota(jnp.int32, (4, 128), 1)
    lane1 = lax.broadcasted_iota(jnp.int32, (1, 128), 1)
    overwrite = (jnp.logical_and(lane < 4, source_side), jnp.logical_and(lane >= 124, source_side))
    overwrite4 = (jnp.logical_and(lane4 < 4, source_side), jnp.logical_and(lane4 >= 124, source_side))

    for i in (0, 3):
        loads[i].wait()
    for d in range(2):
        ys[d] = u[0, :, :, 8 + 12 * d : 12 + 12 * d]
        start(has_y[d], y_copy(0, d))
    for j in range(2):

        @pl.when(has_y[j])
        def _():
            pl.semaphore_wait(ready.at[j], 1)

        for i in range(2):
            start(has_c[i, j], corner_copy(0, i, j))
    for i in (1, 2, 4, 5, 6, 7, 8, 9, 10):
        loads[i].wait()

    source_x = source[0] - at_x * 8
    source_y = source[1] - at_y * 16
    inside = (source_x >= 0) & (source_x < 8) & (source_y >= 0) & (source_y < 16)
    source_flat = jnp.where(inside, (source_x * 16 + source_y) * 256 + source[2], -1)
    where_to = jnp.where(source_side, jnp.where(lane1 == 0, source_flat, -1), cell_v[0])
    row_of = jnp.where(where_to < 0, -1, ((where_to >> 7) & 1) * 128 + (where_to >> 8))
    column_of = where_to & 127
    column_hot = jnp.where(
        lax.broadcasted_iota(jnp.int32, (128, 128), 0) == column_of, 1.0, 0.0
    ).astype(BF16)
    row_hot = lax.broadcasted_iota(jnp.int32, (256, 128), 0) == row_of
    layer = lax.broadcasted_iota(jnp.int32, (128, 256), 0) & 7
    depth_of = jnp.where(layer < 4, layer, 248 + layer)
    spread = jnp.where(
        lax.broadcasted_iota(jnp.int32, (128, 256), 1) == depth_of, 1.0, 0.0
    ).astype(BF16)
    own_row = (
        lax.broadcasted_iota(jnp.int32, (8, 16, 128), 2) >> 3
        == lax.broadcasted_iota(jnp.int32, (8, 16, 128), 1)
    )

    def inject(slot, k):
        sample = jnp.where(source_side, jnp.where(lane1 == 0, -wavelet[k], 0.0), trace_v[k, 0])
        total = None
        for part in split3(sample):
            left = jnp.where(row_hot, part, 0.0).astype(BF16)
            total = add(total, lax.dot_general(
                left, column_hot, (((1,), (1,)), ((), ())), preferred_element_type=F32
            ))
        inj[slot] = total.reshape(2, 8, 16, 128)
        total = None
        for part in split3(strip_v[k]):
            left = jnp.where(own_row, part[:, None, :], 0.0).reshape(128, 128).astype(BF16)
            total = add(total, jnp.dot(left, spread, preferred_element_type=F32))
        for h in range(2):
            dense[slot, h] = total[:, 128 * h : 128 * h + 128].reshape(8, 16, 128)

    def own_part(slot, x):
        lower, upper = u[slot, 0, x, 8:24], u[slot, 1, x, 8:24]
        centre = (lower, upper)
        sums = [inj[slot, h, x] + (3.0 * STENCIL[0]) * centre[h] for h in range(2)]
        for k in range(1, 5):
            depth = shifted_sum(lower, upper, k, lane)
            for h in range(2):
                near = depth[h] + (u[slot, h, x, 8 - k : 24 - k] + u[slot, h, x, 8 + k : 24 + k])
                if x - k >= 0:
                    near = near + u[slot, h, x - k, 8:24]
                if x + k < 8:
                    near = near + u[slot, h, x + k, 8:24]
                sums[h] = sums[h] + W[k] * near
        for h in range(2):
            value = 2.0 * centre[h] - u[1 - slot, h, x, 8:24] + cm[h, x] * sums[h]
            value = jnp.where(overwrite[h], dense[slot, h, x], value)
            t[slot, h, x] = value
            if slot == 0:
                yts[0, h, x] = value[0:4]
                yts[1, h, x] = value[12:16]

    def low_rows(ref):
        total = None
        for m in range(4):
            total = add(total, W[4 - m] * ref[m : m + 8])
        return total

    def high_rows(ref):
        total = None
        for m in range(4):
            total = add(total, W[4 - m] * ref[4 - m : 12 - m])
        return total

    def finish(slot, x, planes):
        d = x // 4
        values = []
        for h in range(2):
            extra = None
            for j in range(4):
                distance = x + 4 - j if d == 0 else 8 + j - x
                if distance <= 4:
                    extra = add(extra, W[distance] * planes(h, j))
            low, high = low_rows(yl.at[h, x]), high_rows(yh.at[h, x])
            first = t[slot, h, x, 0:8] + cm[h, x, 0:8] * (extra[0:8] + low)
            second = t[slot, h, x, 8:16] + cm[h, x, 8:16] * (extra[8:16] + high)
            u[1 - slot, h, x, 8:16] = first
            u[1 - slot, h, x, 16:24] = second
            values.append((first, second))
        return values

    def halo_cross():
        for d in range(2):
            for h in range(2):
                for j in range(4):
                    extra = None
                    for p in range(8):
                        distance = p + 4 - j if d == 0 else 8 + j - p
                        if distance <= 4:
                            extra = add(extra, W[distance] * u[0, h, p, 8:24])
                    hx[d, h, j] = extra
                for x in range(8):
                    extra = None
                    for m in range(4):
                        at = 8 - m if d == 0 else 20 + m
                        extra = add(extra, W[4 - m] * u[0, h, x, at : at + 4])
                    hy[d, h, x] = extra

    def halo_corners(par, i):
        cl[i, :, :, 0:4] = cr[par, i, 0]
        ch[i, :, :, 8:12] = cr[par, i, 1]
        for h in range(2):
            for j in range(4):
                low, high = low_rows(cl.at[i, h, j]), high_rows(ch.at[i, h, j])
                for rows, extra in ((slice(0, 8), low), (slice(8, 16), high)):
                    hx[i, h, j, rows] = xcm[i, h, j, rows] * (hx[i, h, j, rows] + extra)
            for x in range(4 * i, 4 * i + 4):
                for d in range(2):
                    extra = hy[d, h, x]
                    for j in range(4):
                        distance = x + 4 - j if i == 0 else 8 + j - x
                        if distance <= 4:
                            extra = extra + W[distance] * cr[par, i, d, h, j]
                    value = ytr[par, d, h, x] + ycm[d, h, x] * extra
                    if d == 0:
                        yl[h, x, 0:4] = value
                    else:
                        yh[h, x, 8:12] = value

    def send_t(par):
        for d in range(2):
            for x in range(4 * d, 4 * d + 4):
                own_part(0, x)
            start(has_x[d], xt_copy(par, d))
        for d in range(2):
            start(has_y[d], yt_copy(par, d))

    for h in range(2):
        cm[h] = jnp.where(overwrite[h], 0.0, c[h])
    inject(0, 0)
    send_t(0)
    for d in range(2):
        ycs[d] = c[:, :, 12 * d : 12 * d + 4]
        start(has_y[d], yc_copy(d))

    def one_round(half, par):
        first, final = half == 0, half == 1
        more = True if par == 0 else first
        step = 4 * half + 2 * par
        inject(1, step + 1)
        if par == 0:
            inject(0, step + 2)

            @pl.when(final)
            def _():
                image_copy(0).wait()
                image[...] = u[0, group, :, 8:24] * image_in[0]

        else:

            @pl.when(more)
            def _():
                inject(0, step + 2)

        for d in range(2):
            wait_recv(has_y[d], y_copy(par, 1 - d))
        for x in range(8):
            yl[:, x, 0:4] = yr[par, 0, :, x]
            yh[:, x, 8:12] = yr[par, 1, :, x]
        for d in range(2):
            wait_recv(has_x[d], x_copy(par, 1 - d))
            for x in range(4 * d, 4 * d + 4):
                finish(0, x, lambda h, j: xr[par, d, h, j])

        for x in range(8):
            own_part(1, x)
        halo_cross()
        if par == 0:

            @pl.when(first)
            def _():
                for d in range(2):
                    wait_recv(has_x[d], xc_copy(1 - d))
                    wait_recv(has_y[d], yc_copy(1 - d))
                    for h in range(2):
                        xcm[d, h] = jnp.where(overwrite[h], 0.0, xc[d, h])
                        ycm[d, h] = jnp.where(overwrite4[h], 0.0, yc[d, h])
                for d in range(2):
                    wait_send(has_x[d], xc_copy(d))
                    wait_send(has_y[d], yc_copy(d))

        else:

            @pl.when(final)
            def _():
                for h in range(2):
                    later_out[0, :, :, 128 * h : 128 * h + 128] = u[1, h, :, 8:24]

        for d in range(2):
            wait_send(has_x[d], x_copy(par, d))
            wait_send(has_y[d], y_copy(par, d))
        for i, j in corners:
            wait_send(has_c[i, j], corner_copy(par, i, j))
        for d in range(2):
            wait_recv(has_y[d], yt_copy(par, 1 - d))
        for d in range(2):
            for j in range(2):
                wait_recv(has_c[d, j], corner_copy(par, 1 - d, 1 - j))
            halo_corners(par, d)
            wait_recv(has_x[d], xt_copy(par, 1 - d))
            for x in range(4 * d, 4 * d + 4):
                values = finish(1, x, lambda h, j: xtr[par, d, h, j] + hx[d, h, j])
                for h in range(2):
                    ys[0, h, x] = values[h][0][0:4]
                    ys[1, h, x] = values[h][1][4:8]
            for j in range(2):
                start(jnp.logical_and(more, has_c[d, j]), corner_copy(1 - par, d, j))
            start(jnp.logical_and(more, has_x[d]), x_copy(1 - par, d))
        for d in range(2):
            start(jnp.logical_and(more, has_y[d]), y_copy(1 - par, d))
        for d in range(2):
            wait_send(has_x[d], xt_copy(par, d))
            wait_send(has_y[d], yt_copy(par, d))
        if par == 0:
            send_t(1 - par)
        else:

            @pl.when(first)
            def _():
                image_copy(0).start()
                send_t(1 - par)

            @pl.when(final)
            def _():
                image_copy(1).start()

    def two_rounds(half, carry):
        one_round(half, 0)
        one_round(half, 1)
        return carry

    lax.fori_loop(0, 2, two_rounds, 0)
    for h in range(2):
        now_out[0, :, :, 128 * h : 128 * h + 128] = u[0, h, :, 8:24]
    image_copy(1).wait()
    image_out[...] = image[...] + u[0, group, :, 8:24] * image_in[1]


def hand_out(image_in, now_in, later_in, image_out, now_out, later_out, sem):
    pairs = ((now_in, now_out), (later_in, later_out), (image_in, image_out))
    copies = [pltpu.make_async_copy(a, b, sem.at[i]) for i, (a, b) in enumerate(pairs)]
    for copy in copies:
        copy.start()
    for copy in copies:
        copy.wait()


def local(state_now, state_later, courant, strips, traces, receiver_cells, source_point, wavelet):
    any_space = pl.BlockSpec(memory_space=pl.ANY)
    vmem = pl.BlockSpec(memory_space=pltpu.VMEM)
    dma = pltpu.SemaphoreType.DMA
    v = pltpu.VMEM
    results = pl.pallas_call(
        kernel,
        out_shape=(
            v((8, 16, 128), F32),
            v((1, 8, 16, 256), F32),
            v((1, 8, 16, 256), F32),
        ),
        in_specs=[any_space] * 8,
        out_specs=(vmem,) * 3,
        scratch_shapes=[
            v((2, 2, 8, 32, 128), F32),
            v((2, 2, 8, 16, 128), F32),
            v((2, 8, 16, 128), F32),
            v((2, 8, 16, 128), F32),
            v((2, 2, 2, 4, 16, 128), F32),
            v((2, 2, 2, 4, 16, 128), F32),
            v((2, 2, 2, 8, 4, 128), F32),
            v((2, 2, 2, 8, 4, 128), F32),
            v((2, 2, 2, 2, 4, 4, 128), F32),
            v((2, 2, 4, 16, 128), F32),
            v((2, 2, 8, 4, 128), F32),
            v((2, 2, 4, 16, 128), F32),
            v((2, 2, 8, 4, 128), F32),
            v((2, 2, 8, 4, 128), F32),
            v((2, 2, 8, 4, 128), F32),
            v((2, 2, 8, 4, 128), F32),
            v((2, 8, 16, 128), F32),
            v((2, 8, 16, 128), F32),
            v((2, 2, 4, 16, 128), F32),
            v((2, 2, 4, 16, 128), F32),
            v((2, 2, 4, 16, 128), F32),
            v((2, 2, 8, 4, 128), F32),
            v((2, 2, 8, 16, 128), F32),
            v((2, 2, 8, 16, 128), F32),
            v((2, 8, 16, 128), F32),
            v((8, 16, 128), F32),
            v((8, 8, 128), F32),
            v((8, 1, 1, 128), F32),
            v((1, 1, 128), jnp.int32),
            pltpu.SMEM((3,), jnp.int32),
            pltpu.SMEM((8,), F32),
            dma((11,)),
            dma((2,)), dma((2,)), dma((2,)), dma((2,)), dma((2, 2)), dma((2,)), dma((2,)),
            dma((2, 2)), dma((2, 2)), dma((2, 2)), dma((2, 2)), dma((2, 2, 2)), dma((2,)), dma((2,)),
            dma((2,)), dma((2,)),
            pltpu.SemaphoreType.REGULAR((2,)),
        ],
        compiler_params=pltpu.CompilerParams(collective_id=0, has_side_effects=True),
    )(state_now, state_later, courant, strips, traces, receiver_cells, source_point, wavelet)
    return pl.pallas_call(
        hand_out,
        out_shape=tuple(jax.ShapeDtypeStruct(r.shape, F32) for r in results),
        in_specs=[vmem] * 3,
        out_specs=(any_space,) * 3,
        scratch_shapes=[dma((3,))],
    )(*[pltpu.with_memory_space_constraint(r, pltpu.VMEM) for r in results])


def solution(mesh):
    in_specs = (
        P("grp", "gx", "gy", None),
        P("grp", "gx", "gy", None),
        P("gx", "gy", None),
        P(None, "gx", "gy"),
        P(None, "gx", "gy", None),
        P("gx", "gy", None),
        P(),
        P(),
    )
    out_specs = (P("gx", "gy", "grp"), P("grp", "gx", "gy", None), P("grp", "gx", "gy", None))
    return jax.shard_map(local, mesh=mesh, in_specs=in_specs, out_specs=out_specs, check_vma=False)
```

```python
import jax
import jax.numpy as jnp
from jax import lax
from jax.experimental import pallas as pl
from jax.experimental.pallas import tpu as pltpu
from jax.sharding import PartitionSpec as P

STENCIL = (-205.0 / 72.0, 8.0 / 5.0, -1.0 / 5.0, 8.0 / 315.0, -1.0 / 560.0)
W = (None,) + STENCIL[1:]
MESH = pl.DeviceIdType.MESH
F32 = jnp.float32
BF16 = jnp.bfloat16


def split3(value):
    high = value.astype(BF16).astype(F32)
    rest = value - high
    middle = rest.astype(BF16).astype(F32)
    return high, middle, rest - middle


def shifted_sum(lower, upper, k, lane):
    lower_up, upper_up = pltpu.roll(lower, k, 1), pltpu.roll(upper, k, 1)
    lower_down, upper_down = pltpu.roll(lower, 128 - k, 1), pltpu.roll(upper, 128 - k, 1)
    zero = jnp.zeros_like(lower)
    first, last = lane >= k, lane < 128 - k
    return (
        jnp.where(first, lower_up, zero) + jnp.where(last, lower_down, upper_down),
        jnp.where(first, upper_up, lower_up) + jnp.where(last, upper_down, zero),
    )


def add(total, term):
    return term if total is None else total + term


def kernel(
    now, later, courant, strips, traces, cells, source_in, wavelet_in,
    image_out, now_out, later_out,
    u, t, c, cm, xr, xtr, yr, ytr, cr, xc, yc, xcm, ycm, ys, yts, ycs,
    yl, yh, cl, ch, hx, hy, inj, dense, image_in, image,
    strip_v, trace_v, cell_v, source, wavelet,
    load_sem, xs_sem, xts_sem, ys_sem, yts_sem, cs_sem, xcs_sem, ycs_sem,
    xr_sem, xtr_sem, yr_sem, ytr_sem, cr_sem, xcr_sem, ycr_sem, im_send, im_recv, xps_sem, xpr_sem, ready,
):
    group = lax.axis_index("grp")
    at_x = lax.axis_index("gx")
    at_y = lax.axis_index("gy")
    size_x = lax.axis_size("gx")
    size_y = lax.axis_size("gy")
    source_side = group == 0
    has_x = (at_x > 0, at_x < size_x - 1)
    has_y = (at_y > 0, at_y < size_y - 1)
    x_of = (at_x - 1, at_x + 1)
    y_of = (at_y - 1, at_y + 1)
    partner = {"grp": 1 - group}
    corners = [(i, j) for i in range(2) for j in range(2)]
    has_c = {(i, j): jnp.logical_and(has_x[i], has_y[j]) for i, j in corners}

    barrier = pltpu.get_barrier_semaphore()
    count = jnp.int32(1)
    others = [(has_x[d], {"gx": x_of[d]}) for d in range(2)]
    others += [(has_y[d], {"gy": y_of[d]}) for d in range(2)]
    pl.semaphore_signal(barrier, inc=1, device_id=partner, device_id_type=MESH)
    for there, device in others:
        count = count + there.astype(jnp.int32)

        @pl.when(there)
        def _():
            pl.semaphore_signal(barrier, inc=1, device_id=device, device_id_type=MESH)

    loads = []
    for h in range(2):
        zs = pl.ds(128 * h, 128)
        loads.append((now.at[0, :, :, zs], u.at[0, h, :, pl.ds(8, 16)]))
        loads.append((later.at[0, :, :, zs], u.at[1, h, :, pl.ds(8, 16)]))
        loads.append((courant.at[:, :, zs], c.at[h]))
    loads += [(cells, cell_v), (traces, trace_v), (strips, strip_v)]
    loads += [(source_in, source), (wavelet_in, wavelet)]
    loads = [pltpu.make_async_copy(a, b, load_sem.at[i]) for i, (a, b) in enumerate(loads)]
    for copy in loads:
        copy.start()

    def remote(src, dst, send, recv, device):
        return pltpu.make_async_remote_copy(
            src_ref=src, dst_ref=dst, send_sem=send, recv_sem=recv,
            device_id=device, device_id_type=MESH,
        )

    def x_copy(par, d):
        return remote(u.at[0, :, pl.ds(4 * d, 4), pl.ds(8, 16)], xr.at[par, 1 - d],
                      xs_sem.at[d], xr_sem.at[par, 1 - d], {"gx": x_of[d]})

    def xt_copy(par, d):
        return remote(t.at[0, :, pl.ds(4 * d, 4)], xtr.at[par, 1 - d],
                      xts_sem.at[d], xtr_sem.at[par, 1 - d], {"gx": x_of[d]})

    def y_copy(par, d):
        return remote(ys.at[d], yr.at[par, 1 - d],
                      ys_sem.at[d], yr_sem.at[par, 1 - d], {"gy": y_of[d]})

    def yt_copy(par, d):
        return remote(yts.at[d], ytr.at[par, 1 - d],
                      yts_sem.at[d], ytr_sem.at[par, 1 - d], {"gy": y_of[d]})

    def corner_copy(par, i, j):
        return remote(ys.at[j, :, pl.ds(4 * i, 4)], cr.at[par, 1 - i, 1 - j],
                      cs_sem.at[i, j], cr_sem.at[par, 1 - i, 1 - j], {"gx": x_of[i], "gy": y_of[j]})

    def x_first(d, h):
        return remote(now.at[0, pl.ds(4 * d, 4), :, pl.ds(128 * h, 128)], xr.at[0, 1 - d, h],
                      xs_sem.at[d], xr_sem.at[0, 1 - d], {"gx": x_of[d]})

    def xc_first(d):
        mine = pl.ds(pl.multiple_of(128 * group, 128), 128)
        return remote(courant.at[pl.ds(4 * d, 4), :, mine], xc.at[1 - d, group],
                      xcs_sem.at[d], xcr_sem.at[1 - d], {"gx": x_of[d]})

    def xc_pass(d):
        return remote(xc.at[d, group], xc.at[d, group], xps_sem.at[d], xpr_sem.at[d], partner)

    def yc_copy(d):
        return remote(ycs.at[d], yc.at[1 - d], ycs_sem.at[d], ycr_sem.at[1 - d], {"gy": y_of[d]})

    def image_copy(slot):
        return remote(u.at[0, 1 - group, :, pl.ds(8, 16)], image_in.at[slot],
                      im_send.at[slot], im_recv.at[slot], partner)

    def start(there, copy):
        @pl.when(there)
        def _():
            copy.start()

    def wait_recv(there, copy):
        @pl.when(there)
        def _():
            copy.wait_recv()

    def wait_send(there, copy):
        @pl.when(there)
        def _():
            copy.wait_send()

    pl.semaphore_wait(barrier, count)
    for d in range(2):
        start(has_x[d], xc_first(d))
    for d in range(2):
        for h in range(2):
            start(has_x[d], x_first(d, h))
    for d in range(2):

        @pl.when(has_y[d])
        def _():
            pl.semaphore_signal(ready.at[1 - d], inc=1, device_id={"gy": y_of[d]}, device_id_type=MESH)


    for slot in range(2):
        u[slot, :, :, 0:8] = jnp.zeros((2, 8, 8, 128), F32)
        u[slot, :, :, 24:32] = jnp.zeros((2, 8, 8, 128), F32)
    for ref in (yl, yh, cl, ch):
        ref[...] = jnp.zeros_like(ref)
    for d in range(2):

        @pl.when(jnp.logical_not(has_x[d]))
        def _():
            xc[d] = jnp.zeros_like(xc[d])
            for par in range(2):
                xr[par, d] = jnp.zeros_like(xr[par, d])
                xtr[par, d] = jnp.zeros_like(xtr[par, d])

        @pl.when(jnp.logical_not(has_y[d]))
        def _():
            yc[d] = jnp.zeros_like(yc[d])
            for par in range(2):
                yr[par, d] = jnp.zeros_like(yr[par, d])
                ytr[par, d] = jnp.zeros_like(ytr[par, d])

    for i, j in corners:

        @pl.when(jnp.logical_not(has_c[i, j]))
        def _():
            for par in range(2):
                cr[par, i, j] = jnp.zeros_like(cr[par, i, j])

    lane = lax.broadcasted_iota(jnp.int32, (16, 128), 1)
    lane4 = lax.broadcasted_iota(jnp.int32, (4, 128), 1)
    lane1 = lax.broadcasted_iota(jnp.int32, (1, 128), 1)
    overwrite = (jnp.logical_and(lane < 4, source_side), jnp.logical_and(lane >= 124, source_side))
    overwrite4 = (jnp.logical_and(lane4 < 4, source_side), jnp.logical_and(lane4 >= 124, source_side))

    for i in (0, 3):
        loads[i].wait()
    for d in range(2):
        ys[d] = u[0, :, :, 8 + 12 * d : 12 + 12 * d]
        start(has_y[d], y_copy(0, d))
    for j in range(2):

        @pl.when(has_y[j])
        def _():
            pl.semaphore_wait(ready.at[j], 1)

        for i in range(2):
            start(has_c[i, j], corner_copy(0, i, j))
    for i in (1, 2, 4, 5, 6, 7, 8, 9, 10):
        loads[i].wait()

    source_x = source[0] - at_x * 8
    source_y = source[1] - at_y * 16
    inside = (source_x >= 0) & (source_x < 8) & (source_y >= 0) & (source_y < 16)
    source_flat = jnp.where(inside, (source_x * 16 + source_y) * 256 + source[2], -1)
    where_to = jnp.where(source_side, jnp.where(lane1 == 0, source_flat, -1), cell_v[0])
    row_of = jnp.where(where_to < 0, -1, ((where_to >> 7) & 1) * 128 + (where_to >> 8))
    column_of = where_to & 127
    column_hot = jnp.where(
        lax.broadcasted_iota(jnp.int32, (128, 128), 0) == column_of, 1.0, 0.0
    ).astype(BF16)
    row_hot = lax.broadcasted_iota(jnp.int32, (256, 128), 0) == row_of
    layer = lax.broadcasted_iota(jnp.int32, (128, 256), 0) & 7
    depth_of = jnp.where(layer < 4, layer, 248 + layer)
    spread = jnp.where(
        lax.broadcasted_iota(jnp.int32, (128, 256), 1) == depth_of, 1.0, 0.0
    ).astype(BF16)
    own_row = (
        lax.broadcasted_iota(jnp.int32, (8, 16, 128), 2) >> 3
        == lax.broadcasted_iota(jnp.int32, (8, 16, 128), 1)
    )

    def inject(slot, k):
        sample = jnp.where(source_side, jnp.where(lane1 == 0, -wavelet[k], 0.0), trace_v[k, 0])
        total = None
        for part in split3(sample):
            left = jnp.where(row_hot, part, 0.0).astype(BF16)
            total = add(total, lax.dot_general(
                left, column_hot, (((1,), (1,)), ((), ())), preferred_element_type=F32
            ))
        inj[slot] = total.reshape(2, 8, 16, 128)
        total = None
        for part in split3(strip_v[k]):
            left = jnp.where(own_row, part[:, None, :], 0.0).reshape(128, 128).astype(BF16)
            total = add(total, jnp.dot(left, spread, preferred_element_type=F32))
        for h in range(2):
            dense[slot, h] = total[:, 128 * h : 128 * h + 128].reshape(8, 16, 128)

    def own_part(slot, x):
        lower, upper = u[slot, 0, x, 8:24], u[slot, 1, x, 8:24]
        centre = (lower, upper)
        sums = [inj[slot, h, x] + (3.0 * STENCIL[0]) * centre[h] for h in range(2)]
        for k in range(1, 5):
            depth = shifted_sum(lower, upper, k, lane)
            for h in range(2):
                near = depth[h] + (u[slot, h, x, 8 - k : 24 - k] + u[slot, h, x, 8 + k : 24 + k])
                if x - k >= 0:
                    near = near + u[slot, h, x - k, 8:24]
                if x + k < 8:
                    near = near + u[slot, h, x + k, 8:24]
                sums[h] = sums[h] + W[k] * near
        for h in range(2):
            value = 2.0 * centre[h] - u[1 - slot, h, x, 8:24] + cm[h, x] * sums[h]
            value = jnp.where(overwrite[h], dense[slot, h, x], value)
            t[slot, h, x] = value
            if slot == 0:
                yts[0, h, x] = value[0:4]
                yts[1, h, x] = value[12:16]

    def low_rows(ref):
        total = None
        for m in range(4):
            total = add(total, W[4 - m] * ref[m : m + 8])
        return total

    def high_rows(ref):
        total = None
        for m in range(4):
            total = add(total, W[4 - m] * ref[4 - m : 12 - m])
        return total

    def finish(slot, x, planes):
        d = x // 4
        values = []
        for h in range(2):
            extra = None
            for j in range(4):
                distance = x + 4 - j if d == 0 else 8 + j - x
                if distance <= 4:
                    extra = add(extra, W[distance] * planes(h, j))
            low, high = low_rows(yl.at[h, x]), high_rows(yh.at[h, x])
            first = t[slot, h, x, 0:8] + cm[h, x, 0:8] * (extra[0:8] + low)
            second = t[slot, h, x, 8:16] + cm[h, x, 8:16] * (extra[8:16] + high)
            u[1 - slot, h, x, 8:16] = first
            u[1 - slot, h, x, 16:24] = second
            values.append((first, second))
        return values

    def halo_cross():
        for d in range(2):
            for h in range(2):
                for j in range(4):
                    extra = None
                    for p in range(8):
                        distance = p + 4 - j if d == 0 else 8 + j - p
                        if distance <= 4:
                            extra = add(extra, W[distance] * u[0, h, p, 8:24])
                    hx[d, h, j] = extra
                for x in range(8):
                    extra = None
                    for m in range(4):
                        at = 8 - m if d == 0 else 20 + m
                        extra = add(extra, W[4 - m] * u[0, h, x, at : at + 4])
                    hy[d, h, x] = extra

    def halo_corners(par, i):
        cl[i, :, :, 0:4] = cr[par, i, 0]
        ch[i, :, :, 8:12] = cr[par, i, 1]
        for h in range(2):
            for j in range(4):
                low, high = low_rows(cl.at[i, h, j]), high_rows(ch.at[i, h, j])
                for rows, extra in ((slice(0, 8), low), (slice(8, 16), high)):
                    hx[i, h, j, rows] = xcm[i, h, j, rows] * (hx[i, h, j, rows] + extra)
            for x in range(4 * i, 4 * i + 4):
                for d in range(2):
                    extra = hy[d, h, x]
                    for j in range(4):
                        distance = x + 4 - j if i == 0 else 8 + j - x
                        if distance <= 4:
                            extra = extra + W[distance] * cr[par, i, d, h, j]
                    value = ytr[par, d, h, x] + ycm[d, h, x] * extra
                    if d == 0:
                        yl[h, x, 0:4] = value
                    else:
                        yh[h, x, 8:12] = value

    def send_t(par):
        for d in range(2):
            for x in range(4 * d, 4 * d + 4):
                own_part(0, x)
            start(has_x[d], xt_copy(par, d))
        for d in range(2):
            start(has_y[d], yt_copy(par, d))

    for h in range(2):
        cm[h] = jnp.where(overwrite[h], 0.0, c[h])
    inject(0, 0)
    send_t(0)
    for d in range(2):
        ycs[d] = c[:, :, 12 * d : 12 * d + 4]
        start(has_y[d], yc_copy(d))

    def one_round(half, par):
        first, final = half == 0, half == 1
        more = True if par == 0 else first
        step = 4 * half + 2 * par
        inject(1, step + 1)
        if par == 0:
            inject(0, step + 2)

            @pl.when(final)
            def _():
                image_copy(0).wait()
                image[...] = u[0, group, :, 8:24] * image_in[0]

        else:

            @pl.when(more)
            def _():
                inject(0, step + 2)

        if par == 0:

            @pl.when(first)
            def _():
                for d in range(2):
                    wait_recv(has_x[d], xc_first(1 - d))
                    start(has_x[d], xc_pass(d))

        for d in range(2):
            wait_recv(has_y[d], y_copy(par, 1 - d))
        for x in range(8):
            yl[:, x, 0:4] = yr[par, 0, :, x]
            yh[:, x, 8:12] = yr[par, 1, :, x]
        for d in range(2):
            wait_recv(has_x[d], x_copy(par, 1 - d))
            for x in range(4 * d, 4 * d + 4):
                finish(0, x, lambda h, j: xr[par, d, h, j])

        for x in range(8):
            own_part(1, x)
        halo_cross()
        if par == 0:

            @pl.when(first)
            def _():
                for d in range(2):
                    wait_recv(has_x[d], xc_pass(d))
                    wait_recv(has_y[d], yc_copy(1 - d))
                    for h in range(2):
                        xcm[d, h] = jnp.where(overwrite[h], 0.0, xc[d, h])
                        ycm[d, h] = jnp.where(overwrite4[h], 0.0, yc[d, h])
                for d in range(2):
                    wait_send(has_x[d], xc_first(d))
                    wait_send(has_x[d], xc_pass(d))
                    wait_send(has_y[d], yc_copy(d))

        else:

            @pl.when(final)
            def _():
                for h in range(2):
                    later_out[0, :, :, 128 * h : 128 * h + 128] = u[1, h, :, 8:24]

        for d in range(2):
            wait_send(has_x[d], x_copy(par, d))
            wait_send(has_y[d], y_copy(par, d))
        for i, j in corners:
            wait_send(has_c[i, j], corner_copy(par, i, j))
        for d in range(2):
            wait_recv(has_y[d], yt_copy(par, 1 - d))
        for d in range(2):
            for j in range(2):
                wait_recv(has_c[d, j], corner_copy(par, 1 - d, 1 - j))
            halo_corners(par, d)
            wait_recv(has_x[d], xt_copy(par, 1 - d))
            for x in range(4 * d, 4 * d + 4):
                values = finish(1, x, lambda h, j: xtr[par, d, h, j] + hx[d, h, j])
                for h in range(2):
                    ys[0, h, x] = values[h][0][0:4]
                    ys[1, h, x] = values[h][1][4:8]
            for j in range(2):
                start(jnp.logical_and(more, has_c[d, j]), corner_copy(1 - par, d, j))
            start(jnp.logical_and(more, has_x[d]), x_copy(1 - par, d))
        for d in range(2):
            start(jnp.logical_and(more, has_y[d]), y_copy(1 - par, d))
        for d in range(2):
            wait_send(has_x[d], xt_copy(par, d))
            wait_send(has_y[d], yt_copy(par, d))
        if par == 0:
            send_t(1 - par)
        else:

            @pl.when(first)
            def _():
                image_copy(0).start()
                send_t(1 - par)

            @pl.when(final)
            def _():
                image_copy(1).start()

    def two_rounds(half, carry):
        one_round(half, 0)
        one_round(half, 1)
        return carry

    lax.fori_loop(0, 2, two_rounds, 0)
    for h in range(2):
        now_out[0, :, :, 128 * h : 128 * h + 128] = u[0, h, :, 8:24]
    image_copy(1).wait()
    image_out[...] = image[...] + u[0, group, :, 8:24] * image_in[1]


def hand_out(image_in, now_in, later_in, image_out, now_out, later_out, sem):
    pairs = ((now_in, now_out), (later_in, later_out), (image_in, image_out))
    copies = [pltpu.make_async_copy(a, b, sem.at[i]) for i, (a, b) in enumerate(pairs)]
    for copy in copies:
        copy.start()
    for copy in copies:
        copy.wait()


def local(state_now, state_later, courant, strips, traces, receiver_cells, source_point, wavelet):
    any_space = pl.BlockSpec(memory_space=pl.ANY)
    vmem = pl.BlockSpec(memory_space=pltpu.VMEM)
    dma = pltpu.SemaphoreType.DMA
    v = pltpu.VMEM
    results = pl.pallas_call(
        kernel,
        out_shape=(
            v((8, 16, 128), F32),
            v((1, 8, 16, 256), F32),
            v((1, 8, 16, 256), F32),
        ),
        in_specs=[any_space] * 8,
        out_specs=(vmem,) * 3,
        scratch_shapes=[
            v((2, 2, 8, 32, 128), F32),
            v((2, 2, 8, 16, 128), F32),
            v((2, 8, 16, 128), F32),
            v((2, 8, 16, 128), F32),
            v((2, 2, 2, 4, 16, 128), F32),
            v((2, 2, 2, 4, 16, 128), F32),
            v((2, 2, 2, 8, 4, 128), F32),
            v((2, 2, 2, 8, 4, 128), F32),
            v((2, 2, 2, 2, 4, 4, 128), F32),
            v((2, 2, 4, 16, 128), F32),
            v((2, 2, 8, 4, 128), F32),
            v((2, 2, 4, 16, 128), F32),
            v((2, 2, 8, 4, 128), F32),
            v((2, 2, 8, 4, 128), F32),
            v((2, 2, 8, 4, 128), F32),
            v((2, 2, 8, 4, 128), F32),
            v((2, 8, 16, 128), F32),
            v((2, 8, 16, 128), F32),
            v((2, 2, 4, 16, 128), F32),
            v((2, 2, 4, 16, 128), F32),
            v((2, 2, 4, 16, 128), F32),
            v((2, 2, 8, 4, 128), F32),
            v((2, 2, 8, 16, 128), F32),
            v((2, 2, 8, 16, 128), F32),
            v((2, 8, 16, 128), F32),
            v((8, 16, 128), F32),
            v((8, 8, 128), F32),
            v((8, 1, 1, 128), F32),
            v((1, 1, 128), jnp.int32),
            pltpu.SMEM((3,), jnp.int32),
            pltpu.SMEM((8,), F32),
            dma((11,)),
            dma((2,)), dma((2,)), dma((2,)), dma((2,)), dma((2, 2)), dma((2,)), dma((2,)),
            dma((2, 2)), dma((2, 2)), dma((2, 2)), dma((2, 2)), dma((2, 2, 2)), dma((2,)), dma((2,)),
            dma((2,)), dma((2,)), dma((2,)), dma((2,)),
            pltpu.SemaphoreType.REGULAR((2,)),
        ],
        compiler_params=pltpu.CompilerParams(collective_id=0, has_side_effects=True),
    )(state_now, state_later, courant, strips, traces, receiver_cells, source_point, wavelet)
    return pl.pallas_call(
        hand_out,
        out_shape=tuple(jax.ShapeDtypeStruct(r.shape, F32) for r in results),
        in_specs=[vmem] * 3,
        out_specs=(any_space,) * 3,
        scratch_shapes=[dma((3,))],
    )(*[pltpu.with_memory_space_constraint(r, pltpu.VMEM) for r in results])


def solution(mesh):
    in_specs = (
        P("grp", "gx", "gy", None),
        P("grp", "gx", "gy", None),
        P("gx", "gy", None),
        P(None, "gx", "gy"),
        P(None, "gx", "gy", None),
        P("gx", "gy", None),
        P(),
        P(),
    )
    out_specs = (P("gx", "gy", "grp"), P("grp", "gx", "gy", None), P("grp", "gx", "gy", None))
    return jax.shard_map(local, mesh=mesh, in_specs=in_specs, out_specs=out_specs, check_vma=False)
```

```python
import jax
import jax.numpy as jnp
from jax import lax
from jax.experimental import pallas as pl
from jax.experimental.pallas import tpu as pltpu
from jax.sharding import PartitionSpec as P

STENCIL = (-205.0 / 72.0, 8.0 / 5.0, -1.0 / 5.0, 8.0 / 315.0, -1.0 / 560.0)
W = (None,) + STENCIL[1:]
MESH = pl.DeviceIdType.MESH
F32 = jnp.float32
BF16 = jnp.bfloat16


def split3(value):
    high = value.astype(BF16).astype(F32)
    rest = value - high
    middle = rest.astype(BF16).astype(F32)
    return high, middle, rest - middle


def shifted_sum(lower, upper, k, lane):
    lower_up, upper_up = pltpu.roll(lower, k, 1), pltpu.roll(upper, k, 1)
    lower_down, upper_down = pltpu.roll(lower, 128 - k, 1), pltpu.roll(upper, 128 - k, 1)
    zero = jnp.zeros_like(lower)
    first, last = lane >= k, lane < 128 - k
    return (
        jnp.where(first, lower_up, zero) + jnp.where(last, lower_down, upper_down),
        jnp.where(first, upper_up, lower_up) + jnp.where(last, upper_down, zero),
    )


def add(total, term):
    return term if total is None else total + term


def kernel(
    now, later, courant, strips, traces, cells, source_in, wavelet_in,
    image_out, now_out, later_out,
    u, t, c, cm, xr, xtr, yr, ytr, cr, xc, yc, xcm, ycm, ys, yts, ycs,
    yl, yh, cl, ch, hx, hy, inj, dense, image_in, image,
    strip_v, trace_v, cell_v, source, wavelet,
    load_sem, xs_sem, xts_sem, ys_sem, yts_sem, cs_sem, xcs_sem, ycs_sem,
    xr_sem, xtr_sem, yr_sem, ytr_sem, cr_sem, xcr_sem, ycr_sem, im_send, im_recv, xps_sem, xpr_sem, ready,
):
    group = lax.axis_index("grp")
    at_x = lax.axis_index("gx")
    at_y = lax.axis_index("gy")
    size_x = lax.axis_size("gx")
    size_y = lax.axis_size("gy")
    source_side = group == 0
    has_x = (at_x > 0, at_x < size_x - 1)
    has_y = (at_y > 0, at_y < size_y - 1)
    x_of = (at_x - 1, at_x + 1)
    y_of = (at_y - 1, at_y + 1)
    partner = {"grp": 1 - group}
    corners = [(i, j) for i in range(2) for j in range(2)]
    has_c = {(i, j): jnp.logical_and(has_x[i], has_y[j]) for i, j in corners}

    barrier = pltpu.get_barrier_semaphore()
    count = jnp.int32(1)
    others = [(has_x[d], {"gx": x_of[d]}) for d in range(2)]
    others += [(has_y[d], {"gy": y_of[d]}) for d in range(2)]
    pl.semaphore_signal(barrier, inc=1, device_id=partner, device_id_type=MESH)
    for there, device in others:
        count = count + there.astype(jnp.int32)

        @pl.when(there)
        def _():
            pl.semaphore_signal(barrier, inc=1, device_id=device, device_id_type=MESH)

    loads = []
    for h in range(2):
        zs = pl.ds(128 * h, 128)
        loads.append((now.at[0, :, :, zs], u.at[0, h, :, pl.ds(8, 16)]))
        loads.append((later.at[0, :, :, zs], u.at[1, h, :, pl.ds(8, 16)]))
        loads.append((courant.at[:, :, zs], c.at[h]))
    loads += [(cells, cell_v), (traces, trace_v), (strips, strip_v)]
    loads += [(source_in, source), (wavelet_in, wavelet)]
    loads = [pltpu.make_async_copy(a, b, load_sem.at[i]) for i, (a, b) in enumerate(loads)]
    for copy in loads:
        copy.start()

    def remote(src, dst, send, recv, device):
        return pltpu.make_async_remote_copy(
            src_ref=src, dst_ref=dst, send_sem=send, recv_sem=recv,
            device_id=device, device_id_type=MESH,
        )

    def x_copy(par, d):
        return remote(u.at[0, :, pl.ds(4 * d, 4), pl.ds(8, 16)], xr.at[par, 1 - d],
                      xs_sem.at[d], xr_sem.at[par, 1 - d], {"gx": x_of[d]})

    def xt_copy(par, d):
        return remote(t.at[0, :, pl.ds(4 * d, 4)], xtr.at[par, 1 - d],
                      xts_sem.at[d], xtr_sem.at[par, 1 - d], {"gx": x_of[d]})

    def y_copy(par, d):
        return remote(ys.at[d], yr.at[par, 1 - d],
                      ys_sem.at[d], yr_sem.at[par, 1 - d], {"gy": y_of[d]})

    def yt_copy(par, d):
        return remote(yts.at[d], ytr.at[par, 1 - d],
                      yts_sem.at[d], ytr_sem.at[par, 1 - d], {"gy": y_of[d]})

    def y_half(par, e, d):
        return remote(ys.at[e, :, pl.ds(4 * d, 4)], yr.at[par, 1 - e, :, pl.ds(4 * d, 4)],
                      ys_sem.at[e], yr_sem.at[par, 1 - e], {"gy": y_of[e]})

    def corner_copy(par, i, j):
        return remote(ys.at[j, :, pl.ds(4 * i, 4)], cr.at[par, 1 - i, 1 - j],
                      cs_sem.at[i, j], cr_sem.at[par, 1 - i, 1 - j], {"gx": x_of[i], "gy": y_of[j]})

    def x_first(d, h):
        return remote(now.at[0, pl.ds(4 * d, 4), :, pl.ds(128 * h, 128)], xr.at[0, 1 - d, h],
                      xs_sem.at[d], xr_sem.at[0, 1 - d], {"gx": x_of[d]})

    def xc_first(d):
        mine = pl.ds(pl.multiple_of(128 * group, 128), 128)
        return remote(courant.at[pl.ds(4 * d, 4), :, mine], xc.at[1 - d, group],
                      xcs_sem.at[d], xcr_sem.at[1 - d], {"gx": x_of[d]})

    def xc_pass(d):
        return remote(xc.at[d, group], xc.at[d, group], xps_sem.at[d], xpr_sem.at[d], partner)

    def yc_copy(d):
        return remote(ycs.at[d], yc.at[1 - d], ycs_sem.at[d], ycr_sem.at[1 - d], {"gy": y_of[d]})

    def image_copy(slot):
        return remote(u.at[0, 1 - group, :, pl.ds(8, 16)], image_in.at[slot],
                      im_send.at[slot], im_recv.at[slot], partner)

    def image_half(slot, d):
        planes = pl.ds(4 * d, 4)
        return remote(u.at[0, 1 - group, planes, pl.ds(8, 16)], image_in.at[slot, planes],
                      im_send.at[slot], im_recv.at[slot], partner)

    def start(there, copy):
        @pl.when(there)
        def _():
            copy.start()

    def wait_recv(there, copy):
        @pl.when(there)
        def _():
            copy.wait_recv()

    def wait_send(there, copy):
        @pl.when(there)
        def _():
            copy.wait_send()

    pl.semaphore_wait(barrier, count)
    for d in range(2):
        start(has_x[d], xc_first(d))
    for d in range(2):
        for h in range(2):
            start(has_x[d], x_first(d, h))
    for d in range(2):

        @pl.when(has_y[d])
        def _():
            pl.semaphore_signal(ready.at[1 - d], inc=1, device_id={"gy": y_of[d]}, device_id_type=MESH)


    for slot in range(2):
        u[slot, :, :, 0:8] = jnp.zeros((2, 8, 8, 128), F32)
        u[slot, :, :, 24:32] = jnp.zeros((2, 8, 8, 128), F32)
    for ref in (yl, yh, cl, ch):
        ref[...] = jnp.zeros_like(ref)
    for d in range(2):

        @pl.when(jnp.logical_not(has_x[d]))
        def _():
            xc[d] = jnp.zeros_like(xc[d])
            for par in range(2):
                xr[par, d] = jnp.zeros_like(xr[par, d])
                xtr[par, d] = jnp.zeros_like(xtr[par, d])

        @pl.when(jnp.logical_not(has_y[d]))
        def _():
            yc[d] = jnp.zeros_like(yc[d])
            for par in range(2):
                yr[par, d] = jnp.zeros_like(yr[par, d])
                ytr[par, d] = jnp.zeros_like(ytr[par, d])

    for i, j in corners:

        @pl.when(jnp.logical_not(has_c[i, j]))
        def _():
            for par in range(2):
                cr[par, i, j] = jnp.zeros_like(cr[par, i, j])

    lane = lax.broadcasted_iota(jnp.int32, (16, 128), 1)
    lane4 = lax.broadcasted_iota(jnp.int32, (4, 128), 1)
    lane1 = lax.broadcasted_iota(jnp.int32, (1, 128), 1)
    overwrite = (jnp.logical_and(lane < 4, source_side), jnp.logical_and(lane >= 124, source_side))
    overwrite4 = (jnp.logical_and(lane4 < 4, source_side), jnp.logical_and(lane4 >= 124, source_side))

    for i in (0, 3):
        loads[i].wait()
    for d in range(2):
        ys[d] = u[0, :, :, 8 + 12 * d : 12 + 12 * d]
        start(has_y[d], y_copy(0, d))
    for j in range(2):

        @pl.when(has_y[j])
        def _():
            pl.semaphore_wait(ready.at[j], 1)

        for i in range(2):
            start(has_c[i, j], corner_copy(0, i, j))
    for i in (1, 2, 4, 5, 6, 7, 8, 9, 10):
        loads[i].wait()

    source_x = source[0] - at_x * 8
    source_y = source[1] - at_y * 16
    inside = (source_x >= 0) & (source_x < 8) & (source_y >= 0) & (source_y < 16)
    source_flat = jnp.where(inside, (source_x * 16 + source_y) * 256 + source[2], -1)
    where_to = jnp.where(source_side, jnp.where(lane1 == 0, source_flat, -1), cell_v[0])
    row_of = jnp.where(where_to < 0, -1, ((where_to >> 7) & 1) * 128 + (where_to >> 8))
    column_of = where_to & 127
    column_hot = jnp.where(
        lax.broadcasted_iota(jnp.int32, (128, 128), 0) == column_of, 1.0, 0.0
    ).astype(BF16)
    row_hot = lax.broadcasted_iota(jnp.int32, (256, 128), 0) == row_of
    layer = lax.broadcasted_iota(jnp.int32, (128, 256), 0) & 7
    depth_of = jnp.where(layer < 4, layer, 248 + layer)
    spread = jnp.where(
        lax.broadcasted_iota(jnp.int32, (128, 256), 1) == depth_of, 1.0, 0.0
    ).astype(BF16)
    own_row = (
        lax.broadcasted_iota(jnp.int32, (8, 16, 128), 2) >> 3
        == lax.broadcasted_iota(jnp.int32, (8, 16, 128), 1)
    )

    def inject(slot, k):
        sample = jnp.where(source_side, jnp.where(lane1 == 0, -wavelet[k], 0.0), trace_v[k, 0])
        total = None
        for part in split3(sample):
            left = jnp.where(row_hot, part, 0.0).astype(BF16)
            total = add(total, lax.dot_general(
                left, column_hot, (((1,), (1,)), ((), ())), preferred_element_type=F32
            ))
        inj[slot] = total.reshape(2, 8, 16, 128)
        total = None
        for part in split3(strip_v[k]):
            left = jnp.where(own_row, part[:, None, :], 0.0).reshape(128, 128).astype(BF16)
            total = add(total, jnp.dot(left, spread, preferred_element_type=F32))
        for h in range(2):
            dense[slot, h] = total[:, 128 * h : 128 * h + 128].reshape(8, 16, 128)

    def own_part(slot, x):
        lower, upper = u[slot, 0, x, 8:24], u[slot, 1, x, 8:24]
        centre = (lower, upper)
        sums = [inj[slot, h, x] + (3.0 * STENCIL[0]) * centre[h] for h in range(2)]
        for k in range(1, 5):
            depth = shifted_sum(lower, upper, k, lane)
            for h in range(2):
                near = depth[h] + (u[slot, h, x, 8 - k : 24 - k] + u[slot, h, x, 8 + k : 24 + k])
                if x - k >= 0:
                    near = near + u[slot, h, x - k, 8:24]
                if x + k < 8:
                    near = near + u[slot, h, x + k, 8:24]
                sums[h] = sums[h] + W[k] * near
        for h in range(2):
            value = 2.0 * centre[h] - u[1 - slot, h, x, 8:24] + cm[h, x] * sums[h]
            value = jnp.where(overwrite[h], dense[slot, h, x], value)
            t[slot, h, x] = value
            if slot == 0:
                yts[0, h, x] = value[0:4]
                yts[1, h, x] = value[12:16]

    def low_rows(ref):
        total = None
        for m in range(4):
            total = add(total, W[4 - m] * ref[m : m + 8])
        return total

    def high_rows(ref):
        total = None
        for m in range(4):
            total = add(total, W[4 - m] * ref[4 - m : 12 - m])
        return total

    def finish(slot, x, planes):
        d = x // 4
        values = []
        for h in range(2):
            extra = None
            for j in range(4):
                distance = x + 4 - j if d == 0 else 8 + j - x
                if distance <= 4:
                    extra = add(extra, W[distance] * planes(h, j))
            low, high = low_rows(yl.at[h, x]), high_rows(yh.at[h, x])
            first = t[slot, h, x, 0:8] + cm[h, x, 0:8] * (extra[0:8] + low)
            second = t[slot, h, x, 8:16] + cm[h, x, 8:16] * (extra[8:16] + high)
            u[1 - slot, h, x, 8:16] = first
            u[1 - slot, h, x, 16:24] = second
            values.append((first, second))
        return values

    def halo_cross():
        for d in range(2):
            for h in range(2):
                for j in range(4):
                    extra = None
                    for p in range(8):
                        distance = p + 4 - j if d == 0 else 8 + j - p
                        if distance <= 4:
                            extra = add(extra, W[distance] * u[0, h, p, 8:24])
                    hx[d, h, j] = extra
                for x in range(8):
                    extra = None
                    for m in range(4):
                        at = 8 - m if d == 0 else 20 + m
                        extra = add(extra, W[4 - m] * u[0, h, x, at : at + 4])
                    hy[d, h, x] = extra

    def halo_corners(par, i):
        cl[i, :, :, 0:4] = cr[par, i, 0]
        ch[i, :, :, 8:12] = cr[par, i, 1]
        for h in range(2):
            for j in range(4):
                low, high = low_rows(cl.at[i, h, j]), high_rows(ch.at[i, h, j])
                for rows, extra in ((slice(0, 8), low), (slice(8, 16), high)):
                    hx[i, h, j, rows] = xcm[i, h, j, rows] * (hx[i, h, j, rows] + extra)
            for x in range(4 * i, 4 * i + 4):
                for d in range(2):
                    extra = hy[d, h, x]
                    for j in range(4):
                        distance = x + 4 - j if i == 0 else 8 + j - x
                        if distance <= 4:
                            extra = extra + W[distance] * cr[par, i, d, h, j]
                    value = ytr[par, d, h, x] + ycm[d, h, x] * extra
                    if d == 0:
                        yl[h, x, 0:4] = value
                    else:
                        yh[h, x, 8:12] = value

    def send_t(par):
        for d in range(2):
            for x in range(4 * d, 4 * d + 4):
                own_part(0, x)
            start(has_x[d], xt_copy(par, d))
        for d in range(2):
            start(has_y[d], yt_copy(par, d))

    for h in range(2):
        cm[h] = jnp.where(overwrite[h], 0.0, c[h])
    inject(0, 0)
    send_t(0)
    for d in range(2):
        ycs[d] = c[:, :, 12 * d : 12 * d + 4]
        start(has_y[d], yc_copy(d))

    def one_round(half, par):
        first, final = half == 0, half == 1
        more = True if par == 0 else first
        step = 4 * half + 2 * par
        inject(1, step + 1)
        if par == 0:
            inject(0, step + 2)

            @pl.when(final)
            def _():
                image_copy(0).wait()
                image[...] = u[0, group, :, 8:24] * image_in[0]

        else:

            @pl.when(more)
            def _():
                inject(0, step + 2)

        if par == 0:

            @pl.when(first)
            def _():
                for d in range(2):
                    wait_recv(has_x[d], xc_first(1 - d))
                    start(has_x[d], xc_pass(d))

        for d in range(2):
            wait_recv(has_y[d], y_copy(par, 1 - d))
        for x in range(8):
            yl[:, x, 0:4] = yr[par, 0, :, x]
            yh[:, x, 8:12] = yr[par, 1, :, x]
        for d in range(2):
            wait_recv(has_x[d], x_copy(par, 1 - d))
            for x in range(4 * d, 4 * d + 4):
                finish(0, x, lambda h, j: xr[par, d, h, j])

        for x in range(8):
            own_part(1, x)
        halo_cross()
        if par == 0:

            @pl.when(first)
            def _():
                for d in range(2):
                    wait_recv(has_x[d], xc_pass(d))
                    wait_recv(has_y[d], yc_copy(1 - d))
                    for h in range(2):
                        xcm[d, h] = jnp.where(overwrite[h], 0.0, xc[d, h])
                        ycm[d, h] = jnp.where(overwrite4[h], 0.0, yc[d, h])
                for d in range(2):
                    wait_send(has_x[d], xc_first(d))
                    wait_send(has_x[d], xc_pass(d))
                    wait_send(has_y[d], yc_copy(d))

        else:

            @pl.when(final)
            def _():
                for h in range(2):
                    later_out[0, :, :, 128 * h : 128 * h + 128] = u[1, h, :, 8:24]

        for d in range(2):
            wait_send(has_x[d], x_copy(par, d))
            wait_send(has_y[d], y_copy(par, d))
        for i, j in corners:
            wait_send(has_c[i, j], corner_copy(par, i, j))
        for d in range(2):
            wait_recv(has_y[d], yt_copy(par, 1 - d))
        for d in range(2):
            for j in range(2):
                wait_recv(has_c[d, j], corner_copy(par, 1 - d, 1 - j))
            halo_corners(par, d)
            wait_recv(has_x[d], xt_copy(par, 1 - d))
            for x in range(4 * d, 4 * d + 4):
                values = finish(1, x, lambda h, j: xtr[par, d, h, j] + hx[d, h, j])
                for h in range(2):
                    ys[0, h, x] = values[h][0][0:4]
                    ys[1, h, x] = values[h][1][4:8]
            for j in range(2):
                start(jnp.logical_and(more, has_c[d, j]), corner_copy(1 - par, d, j))
            start(jnp.logical_and(more, has_x[d]), x_copy(1 - par, d))
            for e in range(2):
                start(jnp.logical_and(more, has_y[e]), y_half(1 - par, e, d))
            if par == 1:
                start(final, image_half(1, d))
        for d in range(2):
            wait_send(has_x[d], xt_copy(par, d))
            wait_send(has_y[d], yt_copy(par, d))
        if par == 0:
            send_t(1 - par)
        else:

            @pl.when(first)
            def _():
                image_copy(0).start()
                send_t(1 - par)

    def two_rounds(half, carry):
        one_round(half, 0)
        one_round(half, 1)
        return carry

    lax.fori_loop(0, 2, two_rounds, 0)
    for h in range(2):
        now_out[0, :, :, 128 * h : 128 * h + 128] = u[0, h, :, 8:24]
    image_copy(1).wait()
    image_out[...] = image[...] + u[0, group, :, 8:24] * image_in[1]


def hand_out(image_in, now_in, later_in, image_out, now_out, later_out, sem):
    pairs = ((now_in, now_out), (later_in, later_out), (image_in, image_out))
    copies = [pltpu.make_async_copy(a, b, sem.at[i]) for i, (a, b) in enumerate(pairs)]
    for copy in copies:
        copy.start()
    for copy in copies:
        copy.wait()


def local(state_now, state_later, courant, strips, traces, receiver_cells, source_point, wavelet):
    any_space = pl.BlockSpec(memory_space=pl.ANY)
    vmem = pl.BlockSpec(memory_space=pltpu.VMEM)
    dma = pltpu.SemaphoreType.DMA
    v = pltpu.VMEM
    results = pl.pallas_call(
        kernel,
        out_shape=(
            v((8, 16, 128), F32),
            v((1, 8, 16, 256), F32),
            v((1, 8, 16, 256), F32),
        ),
        in_specs=[any_space] * 8,
        out_specs=(vmem,) * 3,
        scratch_shapes=[
            v((2, 2, 8, 32, 128), F32),
            v((2, 2, 8, 16, 128), F32),
            v((2, 8, 16, 128), F32),
            v((2, 8, 16, 128), F32),
            v((2, 2, 2, 4, 16, 128), F32),
            v((2, 2, 2, 4, 16, 128), F32),
            v((2, 2, 2, 8, 4, 128), F32),
            v((2, 2, 2, 8, 4, 128), F32),
            v((2, 2, 2, 2, 4, 4, 128), F32),
            v((2, 2, 4, 16, 128), F32),
            v((2, 2, 8, 4, 128), F32),
            v((2, 2, 4, 16, 128), F32),
            v((2, 2, 8, 4, 128), F32),
            v((2, 2, 8, 4, 128), F32),
            v((2, 2, 8, 4, 128), F32),
            v((2, 2, 8, 4, 128), F32),
            v((2, 8, 16, 128), F32),
            v((2, 8, 16, 128), F32),
            v((2, 2, 4, 16, 128), F32),
            v((2, 2, 4, 16, 128), F32),
            v((2, 2, 4, 16, 128), F32),
            v((2, 2, 8, 4, 128), F32),
            v((2, 2, 8, 16, 128), F32),
            v((2, 2, 8, 16, 128), F32),
            v((2, 8, 16, 128), F32),
            v((8, 16, 128), F32),
            v((8, 8, 128), F32),
            v((8, 1, 1, 128), F32),
            v((1, 1, 128), jnp.int32),
            pltpu.SMEM((3,), jnp.int32),
            pltpu.SMEM((8,), F32),
            dma((11,)),
            dma((2,)), dma((2,)), dma((2,)), dma((2,)), dma((2, 2)), dma((2,)), dma((2,)),
            dma((2, 2)), dma((2, 2)), dma((2, 2)), dma((2, 2)), dma((2, 2, 2)), dma((2,)), dma((2,)),
            dma((2,)), dma((2,)), dma((2,)), dma((2,)),
            pltpu.SemaphoreType.REGULAR((2,)),
        ],
        compiler_params=pltpu.CompilerParams(collective_id=0, has_side_effects=True),
    )(state_now, state_later, courant, strips, traces, receiver_cells, source_point, wavelet)
    return pl.pallas_call(
        hand_out,
        out_shape=tuple(jax.ShapeDtypeStruct(r.shape, F32) for r in results),
        in_specs=[vmem] * 3,
        out_specs=(any_space,) * 3,
        scratch_shapes=[dma((3,))],
    )(*[pltpu.with_memory_space_constraint(r, pltpu.VMEM) for r in results])


def solution(mesh):
    in_specs = (
        P("grp", "gx", "gy", None),
        P("grp", "gx", "gy", None),
        P("gx", "gy", None),
        P(None, "gx", "gy"),
        P(None, "gx", "gy", None),
        P("gx", "gy", None),
        P(),
        P(),
    )
    out_specs = (P("gx", "gy", "grp"), P("grp", "gx", "gy", None), P("grp", "gx", "gy", None))
    return jax.shard_map(local, mesh=mesh, in_specs=in_specs, out_specs=out_specs, check_vma=False)
```
